512 devices in a mesh: clu: 64 (over z, y), col: 8 (over x, core).
Axes of the slice: x: 4, y: 4, z: 16, core: 2. Of those that a mesh axis runs over, the one named last changes fastest.
Arguments:
- near_blocks: float32 [64, 16, 512, 512], P('clu', 'col'), may hold values from -0.25 to 0.25
- diag_block: float32 [64, 512, 512], P('clu', 'col'), as said below
- bases: float32 [64, 512, 512], P('clu', 'col'), as said below
- near_index: int32 [64, 16], replicated, may hold values from 0 to 63, as said below
- near_mask: int32 [64, 16], P('clu'), may hold values from 0 to 1
- parent_map: int32 [64], replicated, may hold values from 0 to 31, as said below
Outputs:
- coupling: float32 [64, 16, 256, 256], P('clu', 'col')
- parent_rows: float32 [64, 256, 512], P('clu', 'col')
- redundant_factor: float32 [64, 256, 256], P('clu', 'col')
The draws below stay inside these ranges and needn't reach their ends.
Inputs may be any that keep to these rules, and one draw needn't show every extreme that they name: `parent_map`: every parent has exactly two children. `near_index`: the slots of cluster i name the clusters (i + d) mod 64 for d = 1 to 7, d = 32 and d = -1 to -8, each offset in exactly one slot, in an order drawn per row; live slots name distinct clusters; exactly one live slot names the cluster's sibling. `diag_block`: each block is symmetric and positive definite. `bases`: each basis change is invertible.
All inputs are finite; a program needn't handle non-finite values.
Results may differ from the reference program's by a relative error of at most 0.0003.
Values sent between devices are 32-bit elements; how exact they have to be, the bound alone decides.
No kernel may reach another device: no remote copies, remote signals or barrier semaphores. Data moves between devices by JAX's collectives and lax.ppermute only.
A program may use at most 64 MiB of HBM per device.

```python
import jax
import jax.numpy as jnp
from jax import lax

LEAF = 512
NEAR = 16
RED = 256
CLUSTERS = 64


def near_tables(key):
    base = jax.random.fold_in(key, 4242)
    key_pair, key_order, key_live = jax.random.split(base, 3)
    cluster_ids = jnp.arange(CLUSTERS, dtype=jnp.int32)
    groups = CLUSTERS // 4
    pair_keys = jax.random.split(key_pair, groups)
    inner = jax.vmap(lambda subkey: jax.random.permutation(subkey, 4))(pair_keys).astype(jnp.int32)
    members = (jnp.arange(groups, dtype=jnp.int32)[:, None] * 4 + inner).reshape(-1)
    position = jnp.zeros((CLUSTERS,), jnp.int32).at[members].set(cluster_ids)
    parent = position // 2
    partner_pos = position + 1 - 2 * (position % 2)
    sibling = members[partner_pos]
    half = NEAR // 2
    far = CLUSTERS // 2
    steps_up = jnp.arange(1, half, dtype=jnp.int32)
    steps_down = jnp.arange(1, half + 1, dtype=jnp.int32)
    offset_table = jnp.concatenate([steps_up, jnp.full((1,), far, jnp.int32), -steps_down])
    row_keys = jax.random.split(key_order, CLUSTERS)
    orders = jax.vmap(lambda subkey: jax.random.permutation(subkey, NEAR))(row_keys).astype(jnp.int32)
    chosen = offset_table[orders]
    near = (cluster_ids[:, None] + chosen) % CLUSTERS
    wanted = (sibling - cluster_ids + CLUSTERS) % CLUSTERS
    is_sibling = (chosen + CLUSTERS) % CLUSTERS == wanted[:, None]
    repeat = (chosen == far) & (far == half)
    coins = jax.random.randint(key_live, (CLUSTERS, NEAR), 0, 4)
    live = ((coins != 0) | is_sibling) & jnp.logical_not(repeat)
    return (near.astype(jnp.int32), live.astype(jnp.int32), parent.astype(jnp.int32))


def draw_near_index(key, part):
    return near_tables(key)[0]


def draw_near_mask(key, part):
    return near_tables(key)[1]


def draw_parent_map(key, part):
    return near_tables(key)[2]


def draw_diag_block(key, part):
    key_raw, key_diag = jax.random.split(jax.random.fold_in(key, 11), 2)
    raw = jax.random.normal(key_raw, (CLUSTERS, LEAF, LEAF), jnp.float32) / jnp.sqrt(jnp.float32(LEAF))
    symmetric = 0.5 * (raw + jnp.swapaxes(raw, 1, 2))
    diagonal = jax.random.uniform(key_diag, (CLUSTERS, LEAF), jnp.float32, 2.0, 4.0)
    matrix = symmetric + diagonal[:, :, None] * jnp.eye(LEAF, dtype=jnp.float32)[None, :, :]
    return matrix


def draw_bases(key, part):
    key_raw, key_diag = jax.random.split(jax.random.fold_in(key, 23), 2)
    noise = 0.35 * jax.random.normal(key_raw, (CLUSTERS, LEAF, LEAF), jnp.float32)
    diagonal = jax.random.uniform(key_diag, (CLUSTERS, LEAF), jnp.float32, 1.0, 2.0)
    return noise / jnp.sqrt(jnp.float32(LEAF)) + diagonal[:, :, None] * jnp.eye(LEAF, dtype=jnp.float32)[None, :, :]


def steps_of(own_key, extent, shards, smallest, top_value):
    def one(dim, blocks):
        draws = jax.random.uniform(jax.random.fold_in(jax.random.fold_in(own_key, 6), dim), (blocks,), jnp.float32, smallest / len(shards), top_value / len(shards))
        return jnp.repeat(jnp.exp(draws), extent[dim] // blocks).reshape((-1,) + (1,) * (len(extent) - dim - 1))

    level = one(*shards[0])
    for cut in shards[1:]:
        level = level * one(*cut)
    return level


def gaussian(rng, shape, width, limit, cuts=(), kind=jnp.bfloat16):
    factor_of = steps_of(rng, shape, cuts, -0.22, 0.18) if cuts else 1.0
    values = jax.random.normal(rng, shape, jnp.float32) * width * factor_of
    return jnp.minimum(jnp.maximum(values, -limit), limit).astype(kind)


def setup_inputs(seed: int = 0) -> dict:
    splits = jax.random.split(jax.random.key(seed), 7)
    near_blocks = gaussian(splits[0], (CLUSTERS, NEAR, LEAF, LEAF), LEAF ** -0.5, 0.25, ((0, 64), (1, 8)), jnp.float32)
    diag_block = draw_diag_block(jax.random.fold_in(splits[6], 71), 0)
    bases = draw_bases(jax.random.fold_in(splits[6], 71), 0)
    near_index = draw_near_index(jax.random.fold_in(splits[6], 71), 0)
    near_mask = draw_near_mask(jax.random.fold_in(splits[6], 71), 0)
    parent_map = draw_parent_map(jax.random.fold_in(splits[6], 71), 0)
    return dict(near_blocks=near_blocks, diag_block=diag_block, bases=bases, near_index=near_index, near_mask=near_mask, parent_map=parent_map)


def solve_lower(factor):
    size = factor.shape[0]
    return lax.linalg.triangular_solve(factor, jnp.eye(size, dtype=factor.dtype), left_side=True, lower=True)

def reference(near_blocks, diag_block, bases, near_index, near_mask, parent_map):
    highest = lax.Precision.HIGHEST
    count = parent_map.shape[0]
    cluster_ids = jnp.arange(count, dtype=jnp.int32)
    same = (parent_map[:, None] == parent_map[None, :]) & (cluster_ids[:, None] != cluster_ids[None, :])
    sibling = jnp.sum(jnp.where(same, cluster_ids[None, :], 0), axis=1).astype(jnp.int32)
    skeleton = bases[:, :, RED:]

    def one_cluster(inputs):
        blocks, diagonal, basis, listed, live, partner, own = inputs
        reduced = jnp.dot(basis.T, jnp.dot(diagonal, basis, precision=highest), precision=highest)
        factor = jnp.linalg.cholesky(reduced[:RED, :RED])
        inverse = solve_lower(factor)
        couple = jnp.dot(inverse, reduced[:RED, RED:], precision=highest)
        schur = reduced[RED:, RED:] - jnp.dot(couple.T, couple, precision=highest)
        partners = skeleton[listed]
        middle = jnp.einsum('kab,kbr->kar', blocks, partners, precision=highest)
        coupled = jnp.einsum('ba,kbr->kar', basis, middle, precision=highest)
        solved = jnp.einsum('xy,kyr->kxr', inverse, coupled[:, :RED], precision=highest)
        weights = live.astype(jnp.float32)
        coupling = (coupled[:, RED:] - jnp.einsum('xs,kxr->ksr', couple, solved, precision=highest)) * weights[:, None, None]
        matches = weights * (listed == partner).astype(jnp.float32)
        side = jnp.einsum('k,kab->ab', matches, coupling, precision=highest)
        first = (own < partner).astype(jnp.float32)
        merged = jnp.concatenate([first * schur + (1.0 - first) * side, (1.0 - first) * schur + first * side], axis=1)
        return (coupling, merged, factor)
    coupling, parent_rows, redundant_factor = lax.map(one_cluster, (near_blocks, diag_block, bases, near_index, near_mask, sibling, cluster_ids))
    return (coupling, parent_rows, redundant_factor)
```

```python
import jax
import jax.numpy as jnp
from jax import lax
from jax.experimental import pallas as pl
from jax.experimental.pallas import tpu as pltpu
from jax.sharding import PartitionSpec as P

RANK = 256
HALF = 128
F32 = jnp.float32
BF16 = jnp.bfloat16
VMEM = pl.BlockSpec(memory_space=pltpu.VMEM)
SMEM = pl.BlockSpec(memory_space=pltpu.SMEM)
ANY = pl.BlockSpec(memory_space=pl.ANY)


def dot_full(a, b, dims=((1,), (0,))):
    return lax.dot_general(
        a, b, (dims, ((), ())), precision=lax.Precision.HIGHEST, preferred_element_type=F32
    )


def split2(x):
    high = x.astype(BF16)
    return high, (x - high.astype(F32)).astype(BF16)


def dot3(a, b, dims=((1,), (0,))):
    def one(x, y):
        return lax.dot_general(x, y, (dims, ((), ())), preferred_element_type=F32)

    return one(a[0], b[0]) + (one(a[0], b[1]) + one(a[1], b[0]))


def split3(x):
    high = x.astype(BF16)
    rest = x - high.astype(F32)
    mid = rest.astype(BF16)
    return high, mid, (rest - mid.astype(F32)).astype(BF16)


def factor_half(work, upper):
    sub = lax.broadcasted_iota(jnp.int32, (8, HALF), 0)

    def spread_lane(x, j):
        return jnp.broadcast_to(x[:, j : j + 1], (8, HALF))

    def spread_row(x, m):
        return jnp.broadcast_to(x[m : m + 1, :], (8, HALF))

    rows_a, rows_w = work[0:8, :HALF], work[0:8, HALF:]
    for group in range(HALF // 8):
        base = 8 * group
        columns = [spread_lane(rows_a, base + j) for j in range(8)]
        cell = {(m, j): spread_row(columns[j], m) for j in range(8) for m in range(j, 8)}
        inv = [None] * 8
        ratio = {}
        for k in range(8):
            inv[k] = 1.0 / cell[k, k]
            for m in range(k + 1, 8):
                ratio[m, k] = cell[m, k] * inv[k]
            for j in range(k + 1, 8):
                for m in range(j, 8):
                    cell[m, j] = cell[m, j] - ratio[m, k] * cell[j, k]
        ra = [spread_row(rows_a, m) for m in range(8)]
        rw = [spread_row(rows_w, m) for m in range(8)]
        for m in range(8):
            for k in range(m):
                ra[m] = ra[m] - ratio[m, k] * ra[k]
                rw[m] = rw[m] - ratio[m, k] * rw[k]
        ua = uw = None
        for m in range(8):
            scale = lax.rsqrt(cell[m, m])
            a, w = ra[m] * scale, rw[m] * scale
            ua = a if ua is None else jnp.where(sub == m, a, ua)
            uw = w if uw is None else jnp.where(sub == m, w, uw)
        upper[base : base + 8, :HALF] = ua
        upper[base : base + 8, HALF:] = uw
        after = base + 8
        if after == HALF:
            break
        next_a, next_w = work[after : after + 8, :HALF], work[after : after + 8, HALF:]
        lead = [spread_lane(next_a, base + k) for k in range(8)]
        for k in range(8):
            for j in range(k):
                lead[k] = lead[k] - lead[j] * ratio[k, j]
        for k in range(8):
            factor = lead[k] * inv[k]
            next_a = next_a - factor * ra[k]
            next_w = next_w - factor * rw[k]
        rows_a, rows_w = next_a, next_w
        low = after + 8
        if low < HALF:
            h, m, l = (x.astype(F32) for x in split3(jnp.concatenate([ua, uw], axis=1)))
            ha, ma, la = h[:, :HALF], m[:, :HALF], l[:, :HALF]
            left = jnp.concatenate([ha, ha, ma, ha, la, ma], axis=0).astype(BF16)
            right = jnp.concatenate([h, m, h, l, h, m], axis=0).astype(BF16)
            step = lax.dot_general(left, right, (((0,), (0,)), ((), ())), preferred_element_type=F32)
            work[low:, :] = work[low:, :] - step[low:, :]


def spread_kernel(diag_ref, bases_ref, out_ref, skeleton_ref):
    rows = diag_ref.shape[0]
    skeleton_ref[...] = bases_ref[:, bases_ref.shape[1] - RANK :]
    diag, bases = diag_ref[...], bases_ref[...]
    for p in range(out_ref.shape[0]):
        out_ref[p, :rows, :] = diag
        out_ref[p, rows:, :] = bases


def order_kernel(own_ref, index_ref, near0, near1, near2, near3, far, out_ref, slot_of, sem):
    own = own_ref[0]
    clusters, slots = index_ref.shape
    for k in range(slots):
        offset = (index_ref[own, k] - own + clusters + slots // 2) % clusters
        slot_of[jnp.where(offset < slots, offset, slots // 2)] = k
    copies = []
    for d in range(slots):
        source = (near0, near1, near2, near3)[d % 4].at[d // 4] if d != slots // 2 else far
        slot = slot_of[d]
        copies.append(pltpu.make_async_copy(source, out_ref.at[slot // 2, slot % 2], sem.at[d]))
    for copy in copies:
        copy.start()
    for copy in copies:
        copy.wait()


def factor_kernel(column_ref, db_ref, solve_ref, schur_ref, factor_ref, work, upper1, upper2, full):
    rows = db_ref.shape[1] // 2
    size = db_ref.shape[0] * rows
    diag = db_ref[:, :rows, :].reshape(size, size)
    basis = db_ref[:, rows:, :].reshape(size, size)
    half = dot_full(diag, basis)
    first = ((0,), (0,))
    reduced = dot_full(half, basis, first)
    red = size - RANK
    ri = lax.broadcasted_iota(jnp.int32, (HALF, HALF), 0)
    ci = lax.broadcasted_iota(jnp.int32, (HALF, HALF), 1)
    eye = (ri == ci).astype(F32)
    work[:, :HALF] = reduced[:HALF, :HALF]
    work[:, HALF:] = eye
    factor_half(work, upper1)
    inv1 = upper1[:, HALF:]
    top = dot_full(inv1, reduced[:HALF, HALF:])
    low_t = top[:, :HALF]
    rest = reduced[HALF:red, HALF:] - dot_full(low_t, top, first)
    work[:, :HALF] = rest[:, :HALF]
    work[:, HALF:] = eye
    factor_half(work, upper2)
    inv2 = upper2[:, HALF:]
    couple1 = top[:, HALF:]
    joint = dot_full(inv2, jnp.concatenate([rest[:, HALF:], dot_full(low_t, inv1, first)], axis=1))
    couple2, cross = joint[:, :RANK], joint[:, RANK:]
    solve_ref[:HALF, :] = dot_full(inv1, couple1, first) - dot_full(cross, couple2, first)
    solve_ref[HALF:, :] = dot_full(inv2, couple2, first)
    column = column_ref[0]
    count = schur_ref.shape[0]
    start = pl.multiple_of(column * count, count)
    full[...] = reduced[red:, red:] - (
        dot_full(couple1, couple1, first) + dot_full(couple2, couple2, first)
    )
    schur_ref[...] = full[pl.ds(start, count), :]
    full[:HALF, :HALF] = jnp.where(ri >= ci, upper1[:, :HALF].T, 0.0)
    full[HALF:, :HALF] = low_t.T
    full[:HALF, HALF:] = jnp.zeros((HALF, HALF), F32)
    full[HALF:, HALF:] = jnp.where(ri >= ci, upper2[:, :HALF].T, 0.0)
    factor_ref[...] = full[pl.ds(start, count), :]


def find_sibling(own, parent_ref):
    parent = parent_ref[own]

    def step(i, found):
        return jnp.where((parent_ref[i] == parent) & (i != own), i, found)

    return lax.fori_loop(0, parent_ref.shape[0], step, jnp.int32(0))


def couple_kernel(
    place_ref, index_ref, mask_ref, parent_ref, near_ref, routed_ref, db_ref, solve_ref, out_ref, side_ref
):
    own, column = place_ref[0], place_ref[1]
    sibling = find_sibling(own, parent_ref)
    rows = db_ref.shape[1] // 2
    size = db_ref.shape[0] * rows
    red = size - RANK
    basis = db_ref[:, rows:, :].reshape(size, size)
    lift = basis[:, red:] - dot_full(basis[:, :red], solve_ref[...])
    lift2 = split2(lift)
    side = jnp.zeros((RANK, RANK), F32)
    for k in range(near_ref.shape[0]):
        slot = column * near_ref.shape[0] + k
        partner = routed_ref[:, k].reshape(size, RANK)
        middle = dot3(split2(near_ref[k]), split2(partner))
        live = mask_ref[0, slot].astype(F32)
        coupling = dot3(lift2, split2(middle), ((0,), (0,))) * live
        out_ref[k] = coupling
        match = jnp.where(index_ref[own, slot] == sibling, live, 0.0)
        side = side + match * coupling
    side_ref[...] = side.reshape(side_ref.shape)


def merge_kernel(place_ref, parent_ref, parts_ref, schur_ref, out_ref):
    own = place_ref[0]
    first = own < find_sibling(own, parent_ref)
    side = parts_ref[0]
    for p in range(1, parts_ref.shape[0]):
        side = side + parts_ref[p]
    schur = schur_ref[...]
    out_ref[:, :RANK] = jnp.where(first, schur, side)
    out_ref[:, RANK:] = jnp.where(first, side, schur)


def shards(near_blocks, diag_block, bases, near_index, near_mask, parent_map):
    columns = lax.axis_size("col")
    clusters = lax.axis_size("clu")
    column = lax.axis_index("col").astype(jnp.int32)
    own = lax.axis_index("clu").astype(jnp.int32)
    place = jnp.stack([own, column])
    rows, size = bases.shape[1:]
    per_device = near_blocks.shape[1]
    shape = jax.ShapeDtypeStruct

    def shift(x, d):
        return lax.ppermute(x, "clu", [((i + d) % clusters, i) for i in range(clusters)])

    spread, skeleton = pl.pallas_call(
        spread_kernel,
        out_shape=(shape((columns, 2 * rows, size), F32), shape((rows, RANK), F32)),
        in_specs=[VMEM] * 2,
        out_specs=(VMEM,) * 2,
        name="spread",
    )(diag_block[0], bases[0])
    down4, up4, down8 = shift(skeleton, -4), shift(skeleton, 4), shift(skeleton, -8)
    db = lax.all_to_all(spread, "col", split_axis=0, concat_axis=0, tiled=False)
    near0 = jnp.stack([down8, down4, skeleton, up4])
    near1, near2, near3 = shift(near0, 1), shift(near0, 2), shift(near0, 3)
    far = shift(skeleton, clusters // 2)
    ordered = pl.pallas_call(
        order_kernel,
        out_shape=shape((columns, per_device, rows, RANK), F32),
        in_specs=[SMEM] * 2 + [VMEM] * 5,
        out_specs=ANY,
        scratch_shapes=[
            pltpu.SMEM((near_index.shape[1],), jnp.int32),
            pltpu.SemaphoreType.DMA((near_index.shape[1],)),
        ],
        name="order",
    )(own[None], near_index, near0, near1, near2, near3, far)
    routed = lax.all_to_all(ordered, "col", split_axis=0, concat_axis=0, tiled=False)
    count = RANK // columns
    solve, schur, factor = pl.pallas_call(
        factor_kernel,
        out_shape=(
            shape((size - RANK, RANK), F32),
            shape((count, RANK), F32),
            shape(((size - RANK) // columns, size - RANK), F32),
        ),
        in_specs=[SMEM, VMEM],
        out_specs=(VMEM,) * 3,
        scratch_shapes=[pltpu.VMEM((HALF, 2 * HALF), F32)] * 3 + [pltpu.VMEM((RANK, RANK), F32)],
        cost_estimate=pl.CostEstimate(flops=6_000_000_000, bytes_accessed=4_000_000, transcendentals=0),
        name="factor",
    )(column[None], db)
    coupling, side = pl.pallas_call(
        couple_kernel,
        out_shape=(shape((per_device, RANK, RANK), F32), shape((columns, count, RANK), F32)),
        in_specs=[SMEM] * 4 + [VMEM] * 4,
        out_specs=(VMEM,) * 2,
        name="couple",
    )(place, near_index, near_mask, parent_map, near_blocks[0], routed, db, solve)
    parts = lax.all_to_all(side, "col", split_axis=0, concat_axis=0, tiled=False)
    parent_rows = pl.pallas_call(
        merge_kernel,
        out_shape=shape((count, 2 * RANK), F32),
        in_specs=[SMEM] * 2 + [VMEM] * 2,
        out_specs=VMEM,
        name="merge",
    )(place, parent_map, parts, schur)
    return coupling[None], parent_rows[None], factor[None]


def solution(mesh):
    in_specs = (
        P("clu", "col", None, None),
        P("clu", "col", None),
        P("clu", "col", None),
        P(),
        P("clu", None),
        P(),
    )
    out_specs = (P("clu", "col", None, None), P("clu", "col", None), P("clu", "col", None))
    return jax.shard_map(shards, mesh=mesh, in_specs=in_specs, out_specs=out_specs, check_vma=False)
```

```python
import jax
import jax.numpy as jnp
from jax import lax
from jax.experimental import pallas as pl
from jax.experimental.pallas import tpu as pltpu
from jax.sharding import PartitionSpec as P


RANK = 256
HALF = 128
F32 = jnp.float32
BF16 = jnp.bfloat16
VMEM = pl.BlockSpec(memory_space=pltpu.VMEM)
SMEM = pl.BlockSpec(memory_space=pltpu.SMEM)
ANY = pl.BlockSpec(memory_space=pl.ANY)
HBM = pl.BlockSpec(memory_space=pltpu.HBM)


def dot_full(a, b, dims=((1,), (0,))):
    return lax.dot_general(
        a, b, (dims, ((), ())), precision=lax.Precision.HIGHEST, preferred_element_type=F32
    )


def split2(x):
    high = x.astype(BF16)
    return high, (x - high.astype(F32)).astype(BF16)


def dot3(a, b, dims=((1,), (0,))):
    def one(x, y):
        return lax.dot_general(x, y, (dims, ((), ())), preferred_element_type=F32)

    return one(a[0], b[0]) + (one(a[0], b[1]) + one(a[1], b[0]))


def split3(x):
    high = x.astype(BF16)
    rest = x - high.astype(F32)
    mid = rest.astype(BF16)
    return high, mid, (rest - mid.astype(F32)).astype(BF16)


def factor_half(work, upper):
    sub = lax.broadcasted_iota(jnp.int32, (8, HALF), 0)

    def spread_lane(x, j):
        return jnp.broadcast_to(x[:, j : j + 1], (8, HALF))

    def spread_row(x, m):
        return jnp.broadcast_to(x[m : m + 1, :], (8, HALF))

    rows_a, rows_w = work[0:8, :HALF], work[0:8, HALF:]
    for group in range(HALF // 8):
        base = 8 * group
        columns = [spread_lane(rows_a, base + j) for j in range(8)]
        cell = {(m, j): spread_row(columns[j], m) for j in range(8) for m in range(j, 8)}
        inv = [None] * 8
        ratio = {}
        for k in range(8):
            inv[k] = 1.0 / cell[k, k]
            for m in range(k + 1, 8):
                ratio[m, k] = cell[m, k] * inv[k]
            for j in range(k + 1, 8):
                for m in range(j, 8):
                    cell[m, j] = cell[m, j] - ratio[m, k] * cell[j, k]
        ra = [spread_row(rows_a, m) for m in range(8)]
        rw = [spread_row(rows_w, m) for m in range(8)]
        for m in range(8):
            for k in range(m):
                ra[m] = ra[m] - ratio[m, k] * ra[k]
                rw[m] = rw[m] - ratio[m, k] * rw[k]
        ua = uw = None
        for m in range(8):
            scale = lax.rsqrt(cell[m, m])
            a, w = ra[m] * scale, rw[m] * scale
            ua = a if ua is None else jnp.where(sub == m, a, ua)
            uw = w if uw is None else jnp.where(sub == m, w, uw)
        upper[base : base + 8, :HALF] = ua
        upper[base : base + 8, HALF:] = uw
        after = base + 8
        if after == HALF:
            break
        next_a, next_w = work[after : after + 8, :HALF], work[after : after + 8, HALF:]
        lead = [spread_lane(next_a, base + k) for k in range(8)]
        for k in range(8):
            for j in range(k):
                lead[k] = lead[k] - lead[j] * ratio[k, j]
        for k in range(8):
            factor = lead[k] * inv[k]
            next_a = next_a - factor * ra[k]
            next_w = next_w - factor * rw[k]
        rows_a, rows_w = next_a, next_w
        low = after + 8
        if low < HALF:
            h, m, l = (x.astype(F32) for x in split3(jnp.concatenate([ua, uw], axis=1)))
            ha, ma, la = h[:, :HALF], m[:, :HALF], l[:, :HALF]
            left = jnp.concatenate([ha, ha, ma, ha, la, ma], axis=0).astype(BF16)
            right = jnp.concatenate([h, m, h, l, h, m], axis=0).astype(BF16)
            step = lax.dot_general(left, right, (((0,), (0,)), ((), ())), preferred_element_type=F32)
            work[low:, :] = work[low:, :] - step[low:, :]


def params(mib):
    return pltpu.CompilerParams(vmem_limit_bytes=mib * 2**20)


def slice_kernel(bases_ref, skeleton_ref, sem):
    source = bases_ref.at[:, pl.ds(bases_ref.shape[1] - RANK, RANK)]
    run_copies([pltpu.make_async_copy(source, skeleton_ref, sem)])


def run_copies(copies):
    for copy in copies:
        copy.start()
    for copy in copies:
        copy.wait()


def spread_kernel(diag_ref, bases_ref, out_ref, sem):
    rows = diag_ref.shape[0]
    copies = []
    for p in range(out_ref.shape[0]):
        for q, ref in enumerate((diag_ref, bases_ref)):
            target = out_ref.at[p, pl.ds(q * rows, rows)]
            copies.append(pltpu.make_async_copy(ref, target, sem.at[p, q]))
    run_copies(copies)


def order_kernel(own_ref, index_ref, near0, near1, near2, near3, far, out_ref, slot_of, sem):
    own = own_ref[0]
    clusters, slots = index_ref.shape
    for k in range(slots):
        offset = (index_ref[own, k] - own + clusters + slots // 2) % clusters
        slot_of[jnp.where(offset < slots, offset, slots // 2)] = k
    copies = []
    for d in range(slots):
        stack = (near0, near1, near2, near3)[d % 4]
        source = far if d == slots // 2 else stack.at[(0, 2, 1, 3)[d // 4]]
        slot = slot_of[d]
        copies.append(pltpu.make_async_copy(source, out_ref.at[slot // 2, slot % 2], sem.at[d]))
    run_copies(copies)


def factor_kernel(column_ref, db_ref, solve_ref, schur_ref, factor_ref, work, upper1, upper2, full):
    rows = db_ref.shape[1] // 2
    size = db_ref.shape[0] * rows
    diag = db_ref[:, :rows, :].reshape(size, size)
    basis = db_ref[:, rows:, :].reshape(size, size)
    half = dot_full(diag, basis)
    first = ((0,), (0,))
    reduced = dot_full(half, basis, first)
    red = size - RANK
    ri = lax.broadcasted_iota(jnp.int32, (HALF, HALF), 0)
    ci = lax.broadcasted_iota(jnp.int32, (HALF, HALF), 1)
    eye = (ri == ci).astype(F32)
    work[:, :HALF] = reduced[:HALF, :HALF]
    work[:, HALF:] = eye
    factor_half(work, upper1)
    inv1 = upper1[:, HALF:]
    top = dot_full(inv1, reduced[:HALF, HALF:])
    low_t = top[:, :HALF]
    rest = reduced[HALF:red, HALF:] - dot_full(low_t, top, first)
    work[:, :HALF] = rest[:, :HALF]
    work[:, HALF:] = eye
    factor_half(work, upper2)
    inv2 = upper2[:, HALF:]
    couple1 = top[:, HALF:]
    joint = dot_full(inv2, jnp.concatenate([rest[:, HALF:], dot_full(low_t, inv1, first)], axis=1))
    couple2, cross = joint[:, :RANK], joint[:, RANK:]
    solve_ref[:HALF, :] = dot_full(inv1, couple1, first) - dot_full(cross, couple2, first)
    solve_ref[HALF:, :] = dot_full(inv2, couple2, first)
    column = column_ref[0]
    count = schur_ref.shape[0]
    start = pl.multiple_of(column * count, count)
    full[...] = reduced[red:, red:] - (
        dot_full(couple1, couple1, first) + dot_full(couple2, couple2, first)
    )
    schur_ref[...] = full[pl.ds(start, count), :]
    full[:HALF, :HALF] = jnp.where(ri >= ci, upper1[:, :HALF].T, 0.0)
    full[HALF:, :HALF] = low_t.T
    full[:HALF, HALF:] = jnp.zeros((HALF, HALF), F32)
    full[HALF:, HALF:] = jnp.where(ri >= ci, upper2[:, :HALF].T, 0.0)
    factor_ref[...] = full[pl.ds(start, count), :]


def find_sibling(own, parent_ref):
    parent = parent_ref[own]

    def step(i, found):
        return jnp.where((parent_ref[i] == parent) & (i != own), i, found)

    return lax.fori_loop(0, parent_ref.shape[0], step, jnp.int32(0), unroll=True)


def couple_kernel(
    place_ref, index_ref, mask_ref, parent_ref, near_ref, routed_ref, db_ref, solve_ref, out_ref, side_ref, block, sem
):
    loads = [pltpu.make_async_copy(near_ref.at[k], block.at[k], sem.at[k]) for k in range(near_ref.shape[0])]
    for load in loads:
        load.start()
    own, column = place_ref[0], place_ref[1]
    sibling = find_sibling(own, parent_ref)
    rows = db_ref.shape[1] // 2
    size = db_ref.shape[0] * rows
    red = size - RANK
    basis = db_ref[:, rows:, :].reshape(size, size)
    lift = basis[:, red:] - dot_full(basis[:, :red], solve_ref[...])
    lift2 = split2(lift)
    side = jnp.zeros((RANK, RANK), F32)
    for k in range(near_ref.shape[0]):
        slot = column * near_ref.shape[0] + k
        partner = routed_ref[:, k].reshape(size, RANK)
        loads[k].wait()
        middle = dot3(split2(block[k]), split2(partner))
        live = mask_ref[0, slot].astype(F32)
        coupling = dot3(lift2, split2(middle), ((0,), (0,))) * live
        out_ref[k] = coupling
        match = jnp.where(index_ref[own, slot] == sibling, live, 0.0)
        side = side + match * coupling
    side_ref[...] = side.reshape(side_ref.shape)


def merge_kernel(place_ref, parent_ref, parts_ref, schur_ref, out_ref):
    own = place_ref[0]
    first = own < find_sibling(own, parent_ref)
    side = parts_ref[0]
    for p in range(1, parts_ref.shape[0]):
        side = side + parts_ref[p]
    schur = schur_ref[...]
    out_ref[:, :RANK] = jnp.where(first, schur, side)
    out_ref[:, RANK:] = jnp.where(first, side, schur)


def shards(near_blocks, diag_block, bases, near_index, near_mask, parent_map):
    columns = lax.axis_size("col")
    clusters = lax.axis_size("clu")
    column = lax.axis_index("col").astype(jnp.int32)
    own = lax.axis_index("clu").astype(jnp.int32)
    place = jnp.stack([own, column])
    rows, size = bases.shape[1:]
    per_device = near_blocks.shape[1]
    shape = jax.ShapeDtypeStruct

    def shift(x, d):
        return lax.ppermute(x, "clu", [((i + d) % clusters, i) for i in range(clusters)])

    skeleton = pl.pallas_call(
        slice_kernel,
        out_shape=shape((rows, RANK), F32),
        in_specs=[HBM],
        out_specs=VMEM,
        scratch_shapes=[pltpu.SemaphoreType.DMA],
        compiler_params=params(4),
        name="skeleton",
    )(pltpu.with_memory_space_constraint(bases[0], pltpu.HBM))
    down8 = shift(skeleton, -8)
    far = shift(skeleton, clusters // 2)
    pair = jnp.stack([down8, skeleton])
    up4 = shift(pair, 4)
    spread = pl.pallas_call(
        spread_kernel,
        out_shape=pltpu.HBM((columns, 2 * rows, size), F32),
        in_specs=[VMEM] * 2,
        out_specs=HBM,
        scratch_shapes=[pltpu.SemaphoreType.DMA((columns, 2))],
        compiler_params=params(4),
        name="spread",
    )(diag_block[0], bases[0])
    db = lax.all_to_all(spread, "col", split_axis=0, concat_axis=0, tiled=False)
    near0 = jnp.concatenate([pair, up4], axis=0)
    near1 = shift(near0, 1)
    near2 = shift(near0, 2)
    near3 = shift(near0, 3)
    ordered = pl.pallas_call(
        order_kernel,
        out_shape=pltpu.HBM((columns, per_device, rows, RANK), F32),
        in_specs=[SMEM] * 2 + [ANY] * 5,
        out_specs=HBM,
        compiler_params=params(2),
        scratch_shapes=[
            pltpu.SMEM((near_index.shape[1],), jnp.int32),
            pltpu.SemaphoreType.DMA((near_index.shape[1],)),
        ],
        name="order",
    )(own[None], near_index, near0, near1, near2, near3, far)
    routed = lax.all_to_all(ordered, "col", split_axis=0, concat_axis=0, tiled=False)
    count = RANK // columns
    solve, schur, factor = pl.pallas_call(
        factor_kernel,
        out_shape=(
            shape((size - RANK, RANK), F32),
            shape((count, RANK), F32),
            shape(((size - RANK) // columns, size - RANK), F32),
        ),
        in_specs=[SMEM, VMEM],
        out_specs=(VMEM,) * 3,
        scratch_shapes=[pltpu.VMEM((HALF, 2 * HALF), F32)] * 3 + [pltpu.VMEM((RANK, RANK), F32)],
        cost_estimate=pl.CostEstimate(flops=6_000_000_000, bytes_accessed=4_000_000, transcendentals=0),
        compiler_params=params(24),
        name="factor",
    )(column[None], db)
    coupling, side = pl.pallas_call(
        couple_kernel,
        out_shape=(shape((per_device, RANK, RANK), F32), shape((columns, count, RANK), F32)),
        in_specs=[SMEM] * 4 + [HBM] + [VMEM] * 3,
        out_specs=(VMEM,) * 2,
        scratch_shapes=[
            pltpu.VMEM(near_blocks.shape[1:], F32),
            pltpu.SemaphoreType.DMA((per_device,)),
        ],
        compiler_params=params(24),
        name="couple",
    )(
        place,
        near_index,
        near_mask,
        parent_map,
        pltpu.with_memory_space_constraint(near_blocks[0], pltpu.HBM),
        routed,
        db,
        solve,
    )
    parts = lax.all_to_all(side, "col", split_axis=0, concat_axis=0, tiled=False)
    parent_rows = pl.pallas_call(
        merge_kernel,
        out_shape=shape((count, 2 * RANK), F32),
        in_specs=[SMEM] * 2 + [VMEM] * 2,
        out_specs=VMEM,
        compiler_params=params(4),
        name="merge",
    )(place, parent_map, parts, schur)
    return coupling[None], parent_rows[None], factor[None]


def solution(mesh):
    in_specs = (
        P("clu", "col", None, None),
        P("clu", "col", None),
        P("clu", "col", None),
        P(),
        P("clu", None),
        P(),
    )
    out_specs = (P("clu", "col", None, None), P("clu", "col", None), P("clu", "col", None))
    return jax.shard_map(shards, mesh=mesh, in_specs=in_specs, out_specs=out_specs, check_vma=False)
```

```python
import jax
import jax.numpy as jnp
from jax import lax
from jax.experimental import pallas as pl
from jax.experimental.pallas import tpu as pltpu
from jax.sharding import PartitionSpec as P


RANK = 256
HALF = 128
F32 = jnp.float32
BF16 = jnp.bfloat16
VMEM = pl.BlockSpec(memory_space=pltpu.VMEM)
SMEM = pl.BlockSpec(memory_space=pltpu.SMEM)
ANY = pl.BlockSpec(memory_space=pl.ANY)
HBM = pl.BlockSpec(memory_space=pltpu.HBM)


def dot_full(a, b, dims=((1,), (0,))):
    return lax.dot_general(
        a, b, (dims, ((), ())), precision=lax.Precision.HIGHEST, preferred_element_type=F32
    )


def split2(x):
    high = x.astype(BF16)
    return high, (x - high.astype(F32)).astype(BF16)


def dot3(a, b, dims=((1,), (0,))):
    def one(x, y):
        return lax.dot_general(x, y, (dims, ((), ())), preferred_element_type=F32)

    return one(a[0], b[0]) + (one(a[0], b[1]) + one(a[1], b[0]))


def split3(x):
    high = x.astype(BF16)
    rest = x - high.astype(F32)
    mid = rest.astype(BF16)
    return high, mid, (rest - mid.astype(F32)).astype(BF16)


def factor_half(work, upper):
    sub = lax.broadcasted_iota(jnp.int32, (8, HALF), 0)

    def spread_lane(x, j):
        return jnp.broadcast_to(x[:, j : j + 1], (8, HALF))

    def spread_row(x, m):
        return jnp.broadcast_to(x[m : m + 1, :], (8, HALF))

    rows_a, rows_w = work[0:8, :HALF], work[0:8, HALF:]
    for group in range(HALF // 8):
        base = 8 * group
        columns = [spread_lane(rows_a, base + j) for j in range(8)]
        cell = {(m, j): spread_row(columns[j], m) for j in range(8) for m in range(j, 8)}
        inv = [None] * 8
        ratio = {}
        for k in range(8):
            inv[k] = 1.0 / cell[k, k]
            for m in range(k + 1, 8):
                ratio[m, k] = cell[m, k] * inv[k]
            for j in range(k + 1, 8):
                for m in range(j, 8):
                    cell[m, j] = cell[m, j] - ratio[m, k] * cell[j, k]
        ra = [spread_row(rows_a, m) for m in range(8)]
        rw = [spread_row(rows_w, m) for m in range(8)]
        for m in range(8):
            for k in range(m):
                ra[m] = ra[m] - ratio[m, k] * ra[k]
                rw[m] = rw[m] - ratio[m, k] * rw[k]
        ua = uw = None
        for m in range(8):
            scale = lax.rsqrt(cell[m, m])
            a, w = ra[m] * scale, rw[m] * scale
            ua = a if ua is None else jnp.where(sub == m, a, ua)
            uw = w if uw is None else jnp.where(sub == m, w, uw)
        upper[base : base + 8, :HALF] = ua
        upper[base : base + 8, HALF:] = uw
        after = base + 8
        if after == HALF:
            break
        next_a, next_w = work[after : after + 8, :HALF], work[after : after + 8, HALF:]
        lead = [spread_lane(next_a, base + k) for k in range(8)]
        for k in range(8):
            for j in range(k):
                lead[k] = lead[k] - lead[j] * ratio[k, j]
        for k in range(8):
            factor = lead[k] * inv[k]
            next_a = next_a - factor * ra[k]
            next_w = next_w - factor * rw[k]
        rows_a, rows_w = next_a, next_w
        low = after + 8
        if low < HALF:
            h, m, l = (x.astype(F32) for x in split3(jnp.concatenate([ua, uw], axis=1)))
            ha, ma, la = h[:, :HALF], m[:, :HALF], l[:, :HALF]
            left = jnp.concatenate([ha, ha, ma, ha, la, ma], axis=0).astype(BF16)
            right = jnp.concatenate([h, m, h, l, h, m], axis=0).astype(BF16)
            step = lax.dot_general(left, right, (((0,), (0,)), ((), ())), preferred_element_type=F32)
            work[low:, :] = work[low:, :] - step[low:, :]


def params(mib):
    return pltpu.CompilerParams(vmem_limit_bytes=mib * 2**20)


def keep_out(x):
    return pltpu.with_memory_space_constraint(x, pltpu.HBM)


def slice_kernel(bases_ref, skeleton_ref, sem):
    source = bases_ref.at[:, pl.ds(bases_ref.shape[1] - RANK, RANK)]
    run_copies([pltpu.make_async_copy(source, skeleton_ref, sem)])


def run_copies(copies):
    for copy in copies:
        copy.start()
    for copy in copies:
        copy.wait()


def spread_kernel(diag_ref, bases_ref, out_ref, both, sem):
    rows = diag_ref.shape[0]
    pair = (diag_ref, bases_ref)
    run_copies(
        [pltpu.make_async_copy(ref, both.at[pl.ds(q * rows, rows)], sem.at[q]) for q, ref in enumerate(pair)]
    )
    run_copies([pltpu.make_async_copy(both, out_ref.at[p], sem.at[p]) for p in range(out_ref.shape[0])])


def order_kernel(own_ref, index_ref, near0, near1, near2, near3, far, out_ref, slot_of, sem):
    own = own_ref[0]
    clusters, slots = index_ref.shape
    for k in range(slots):
        offset = (index_ref[own, k] - own + clusters + slots // 2) % clusters
        slot_of[jnp.where(offset < slots, offset, slots // 2)] = k
    copies = []
    for d in range(slots):
        stack = (near0, near1, near2, near3)[d % 4]
        source = far if d == slots // 2 else stack.at[(0, 2, 1, 3)[d // 4]]
        slot = slot_of[d]
        copies.append(pltpu.make_async_copy(source, out_ref.at[slot // 2, slot % 2], sem.at[d]))
    run_copies(copies)


def factor_kernel(
    column_ref, db_ref, high_ref, low_ref, schur_ref, factor_ref, work, upper1, upper2, full, solve_ref
):
    rows = db_ref.shape[1] // 2
    size = db_ref.shape[0] * rows
    diag = db_ref[:, :rows, :].reshape(size, size)
    basis = db_ref[:, rows:, :].reshape(size, size)
    first = ((0,), (0,))
    red = size - RANK
    reduced = dot_full(dot_full(diag, basis[:, :red]), basis, first)
    skeleton = split2(basis[:, red:])
    corner = dot3(skeleton, split2(dot3(split2(diag), skeleton)), first)
    ri = lax.broadcasted_iota(jnp.int32, (HALF, HALF), 0)
    ci = lax.broadcasted_iota(jnp.int32, (HALF, HALF), 1)
    eye = (ri == ci).astype(F32)
    work[:, :HALF] = reduced[:HALF, :HALF]
    work[:, HALF:] = eye
    factor_half(work, upper1)
    inv1 = upper1[:, HALF:]
    top = dot_full(inv1, reduced[:HALF, HALF:])
    low_t = top[:, :HALF]
    rest = reduced[HALF:red, HALF:] - dot_full(low_t, top, first)
    work[:, :HALF] = rest[:, :HALF]
    work[:, HALF:] = eye
    factor_half(work, upper2)
    inv2 = upper2[:, HALF:]
    couple1 = top[:, HALF:]
    joint = dot_full(inv2, jnp.concatenate([rest[:, HALF:], dot_full(low_t, inv1, first)], axis=1))
    couple2, cross = joint[:, :RANK], joint[:, RANK:]
    solve_ref[:HALF, :] = dot_full(inv1, couple1, first) - dot_full(cross, couple2, first)
    solve_ref[HALF:, :] = dot_full(inv2, couple2, first)
    lift = basis[:, red:] - dot3(split2(basis[:, :red]), split2(solve_ref[...]))
    high_ref[...], low_ref[...] = split2(lift)
    column = column_ref[0]
    count = schur_ref.shape[0]
    start = pl.multiple_of(column * count, count)
    full[...] = corner - (
        dot_full(couple1, couple1, first) + dot_full(couple2, couple2, first)
    )
    schur_ref[...] = full[pl.ds(start, count), :]
    full[:HALF, :HALF] = jnp.where(ri >= ci, upper1[:, :HALF].T, 0.0)
    full[HALF:, :HALF] = low_t.T
    full[:HALF, HALF:] = jnp.zeros((HALF, HALF), F32)
    full[HALF:, HALF:] = jnp.where(ri >= ci, upper2[:, :HALF].T, 0.0)
    factor_ref[...] = full[pl.ds(start, count), :]


def find_sibling(own, parent_ref):
    parent = parent_ref[own]

    def step(i, found):
        return jnp.where((parent_ref[i] == parent) & (i != own), i, found)

    return lax.fori_loop(0, parent_ref.shape[0], step, jnp.int32(0), unroll=True)


def project_kernel(near_ref, high_ref, low_ref, out_high, out_low, block, sem):
    count = near_ref.shape[0]
    loads = [pltpu.make_async_copy(near_ref.at[k], block.at[k], sem.at[k]) for k in range(count)]
    for load in loads:
        load.start()
    lift = high_ref[...], low_ref[...]
    for k in range(count):
        loads[k].wait()
        out_high[k], out_low[k] = split2(dot3(lift, split2(block[k]), ((0,), (0,))))


def slot_product(high_ref, low_ref, routed_ref, k):
    size = high_ref.shape[2]
    partner = routed_ref[:, k].reshape(size, RANK)
    return dot3((high_ref[k], low_ref[k]), split2(partner))


def side_kernel(place_ref, index_ref, mask_ref, parent_ref, high_ref, low_ref, routed_ref, side_ref):
    own, column = place_ref[0], place_ref[1]
    sibling = find_sibling(own, parent_ref)
    side_ref[...] = jnp.zeros_like(side_ref)
    count = high_ref.shape[0]
    for k in range(count):
        slot = column * count + k

        @pl.when((mask_ref[0, slot] != 0) & (index_ref[own, slot] == sibling))
        def _():
            side_ref[...] = slot_product(high_ref, low_ref, routed_ref, k).reshape(side_ref.shape)


def couple_kernel(place_ref, mask_ref, high_ref, low_ref, routed_ref, out_ref):
    count = high_ref.shape[0]
    for k in range(count):
        live = mask_ref[0, place_ref[1] * count + k].astype(F32)
        out_ref[k] = slot_product(high_ref, low_ref, routed_ref, k) * live


def merge_kernel(place_ref, parent_ref, parts_ref, schur_ref, out_ref):
    own = place_ref[0]
    first = own < find_sibling(own, parent_ref)
    side = parts_ref[0]
    for p in range(1, parts_ref.shape[0]):
        side = side + parts_ref[p]
    schur = schur_ref[...]
    out_ref[:, :RANK] = jnp.where(first, schur, side)
    out_ref[:, RANK:] = jnp.where(first, side, schur)


def shards(near_blocks, diag_block, bases, near_index, near_mask, parent_map):
    columns = lax.axis_size("col")
    clusters = lax.axis_size("clu")
    column = lax.axis_index("col").astype(jnp.int32)
    own = lax.axis_index("clu").astype(jnp.int32)
    place = jnp.stack([own, column])
    rows, size = bases.shape[1:]
    per_device = near_blocks.shape[1]
    shape = jax.ShapeDtypeStruct

    def shift(x, d):
        return lax.ppermute(x, "clu", [((i + d) % clusters, i) for i in range(clusters)])

    skeleton = pl.pallas_call(
        slice_kernel,
        out_shape=shape((rows, RANK), F32),
        in_specs=[HBM],
        out_specs=VMEM,
        scratch_shapes=[pltpu.SemaphoreType.DMA],
        compiler_params=params(4),
        name="skeleton",
    )(keep_out(bases[0]))
    down8 = shift(skeleton, -8)
    far = shift(skeleton, clusters // 2)
    pair = jnp.stack([down8, skeleton])
    up4 = shift(pair, 4)
    spread = pl.pallas_call(
        spread_kernel,
        out_shape=pltpu.HBM((columns, 2 * rows, size), F32),
        in_specs=[HBM] * 2,
        out_specs=HBM,
        scratch_shapes=[pltpu.VMEM((2 * rows, size), F32), pltpu.SemaphoreType.DMA((columns,))],
        compiler_params=params(4),
        name="spread",
    )(keep_out(diag_block[0]), keep_out(bases[0]))
    db = lax.all_to_all(spread, "col", split_axis=0, concat_axis=0, tiled=False)
    near0 = jnp.concatenate([pair, up4], axis=0)
    near1 = shift(near0, 1)
    near2 = shift(near0, 2)
    near3 = shift(near0, 3)
    ordered = pl.pallas_call(
        order_kernel,
        out_shape=pltpu.HBM((columns, per_device, rows, RANK), F32),
        in_specs=[SMEM] * 2 + [ANY] * 5,
        out_specs=HBM,
        compiler_params=params(2),
        scratch_shapes=[
            pltpu.SMEM((near_index.shape[1],), jnp.int32),
            pltpu.SemaphoreType.DMA((near_index.shape[1],)),
        ],
        name="order",
    )(own[None], near_index, near0, near1, near2, near3, far)
    routed = lax.all_to_all(ordered, "col", split_axis=0, concat_axis=0, tiled=False)
    count = RANK // columns
    high, low, schur, factor = pl.pallas_call(
        factor_kernel,
        out_shape=(
            shape((size, RANK), BF16),
            shape((size, RANK), BF16),
            shape((count, RANK), F32),
            shape(((size - RANK) // columns, size - RANK), F32),
        ),
        in_specs=[SMEM, VMEM],
        out_specs=(VMEM,) * 4,
        scratch_shapes=[pltpu.VMEM((HALF, 2 * HALF), F32)] * 3 + [pltpu.VMEM((RANK, RANK), F32)] * 2,
        cost_estimate=pl.CostEstimate(flops=6_000_000_000, bytes_accessed=4_000_000, transcendentals=0),
        compiler_params=params(24),
        name="factor",
    )(column[None], db)
    projected = (per_device, RANK, size)
    rows_high, rows_low = pl.pallas_call(
        project_kernel,
        out_shape=(shape(projected, BF16),) * 2,
        in_specs=[HBM] + [VMEM] * 2,
        out_specs=(VMEM,) * 2,
        scratch_shapes=[
            pltpu.VMEM(near_blocks.shape[1:], F32),
            pltpu.SemaphoreType.DMA((per_device,)),
        ],
        cost_estimate=pl.CostEstimate(flops=1_000_000_000, bytes_accessed=4_000_000, transcendentals=0),
        compiler_params=params(16),
        name="project",
    )(keep_out(near_blocks[0]), high, low)
    side = pl.pallas_call(
        side_kernel,
        out_shape=shape((columns, count, RANK), F32),
        in_specs=[SMEM] * 4 + [VMEM] * 3,
        out_specs=VMEM,
        cost_estimate=pl.CostEstimate(flops=200_000_000, bytes_accessed=2_000_000, transcendentals=0),
        compiler_params=params(8),
        name="side",
    )(place, near_index, near_mask, parent_map, rows_high, rows_low, routed)
    parts = lax.all_to_all(side, "col", split_axis=0, concat_axis=0, tiled=False)
    coupling = pl.pallas_call(
        couple_kernel,
        out_shape=shape((per_device, RANK, RANK), F32),
        in_specs=[SMEM] * 2 + [VMEM] * 3,
        out_specs=VMEM,
        cost_estimate=pl.CostEstimate(flops=400_000_000, bytes_accessed=4_000_000, transcendentals=0),
        compiler_params=params(8),
        name="couple",
    )(place, near_mask, rows_high, rows_low, routed)
    parent_rows = pl.pallas_call(
        merge_kernel,
        out_shape=shape((count, 2 * RANK), F32),
        in_specs=[SMEM] * 2 + [VMEM] * 2,
        out_specs=VMEM,
        compiler_params=params(4),
        name="merge",
    )(place, parent_map, parts, schur)
    return coupling[None], parent_rows[None], factor[None]


def solution(mesh):
    in_specs = (
        P("clu", "col", None, None),
        P("clu", "col", None),
        P("clu", "col", None),
        P(),
        P("clu", None),
        P(),
    )
    out_specs = (P("clu", "col", None, None), P("clu", "col", None), P("clu", "col", None))
    return jax.shard_map(shards, mesh=mesh, in_specs=in_specs, out_specs=out_specs, check_vma=False)
```

```python
import jax
import jax.numpy as jnp
from jax import lax
from jax.experimental import pallas as pl
from jax.experimental.pallas import tpu as pltpu
from jax.sharding import PartitionSpec as P


RANK = 256
HALF = 128
F32 = jnp.float32
BF16 = jnp.bfloat16
VMEM = pl.BlockSpec(memory_space=pltpu.VMEM)
SMEM = pl.BlockSpec(memory_space=pltpu.SMEM)
ANY = pl.BlockSpec(memory_space=pl.ANY)
HBM = pl.BlockSpec(memory_space=pltpu.HBM)


def dot_full(a, b, dims=((1,), (0,))):
    return lax.dot_general(
        a, b, (dims, ((), ())), precision=lax.Precision.HIGHEST, preferred_element_type=F32
    )


def split2(x):
    high = x.astype(BF16)
    return high, (x - high.astype(F32)).astype(BF16)


def dot3(a, b, dims=((1,), (0,))):
    def one(x, y):
        return lax.dot_general(x, y, (dims, ((), ())), preferred_element_type=F32)

    return one(a[0], b[0]) + (one(a[0], b[1]) + one(a[1], b[0]))


def split3(x):
    high = x.astype(BF16)
    rest = x - high.astype(F32)
    mid = rest.astype(BF16)
    return high, mid, (rest - mid.astype(F32)).astype(BF16)


def factor_half(work, upper):
    sub = lax.broadcasted_iota(jnp.int32, (8, HALF), 0)

    def spread_lane(x, j):
        return jnp.broadcast_to(x[:, j : j + 1], (8, HALF))

    def spread_row(x, m):
        return jnp.broadcast_to(x[m : m + 1, :], (8, HALF))

    rows_a, rows_w = work[0:8, :HALF], work[0:8, HALF:]
    for group in range(HALF // 8):
        base = 8 * group
        columns = [spread_lane(rows_a, base + j) for j in range(8)]
        cell = {(m, j): spread_row(columns[j], m) for j in range(8) for m in range(j, 8)}
        inv = [None] * 8
        ratio = {}
        for k in range(8):
            inv[k] = 1.0 / cell[k, k]
            for m in range(k + 1, 8):
                ratio[m, k] = cell[m, k] * inv[k]
            for j in range(k + 1, 8):
                for m in range(j, 8):
                    cell[m, j] = cell[m, j] - ratio[m, k] * cell[j, k]
        ra = [spread_row(rows_a, m) for m in range(8)]
        rw = [spread_row(rows_w, m) for m in range(8)]
        for m in range(8):
            for k in range(m):
                ra[m] = ra[m] - ratio[m, k] * ra[k]
                rw[m] = rw[m] - ratio[m, k] * rw[k]
        ua = uw = None
        for m in range(8):
            scale = lax.rsqrt(cell[m, m])
            a, w = ra[m] * scale, rw[m] * scale
            ua = a if ua is None else jnp.where(sub == m, a, ua)
            uw = w if uw is None else jnp.where(sub == m, w, uw)
        upper[base : base + 8, :HALF] = ua
        upper[base : base + 8, HALF:] = uw
        after = base + 8
        if after == HALF:
            break
        next_a, next_w = work[after : after + 8, :HALF], work[after : after + 8, HALF:]
        lead = [spread_lane(next_a, base + k) for k in range(8)]
        for k in range(8):
            for j in range(k):
                lead[k] = lead[k] - lead[j] * ratio[k, j]
        for k in range(8):
            factor = lead[k] * inv[k]
            next_a = next_a - factor * ra[k]
            next_w = next_w - factor * rw[k]
        rows_a, rows_w = next_a, next_w
        low = after + 8
        if low < HALF:
            h, m, l = (x.astype(F32) for x in split3(jnp.concatenate([ua, uw], axis=1)))
            ha, ma, la = h[:, :HALF], m[:, :HALF], l[:, :HALF]
            left = jnp.concatenate([ha, ha, ma, ha, la, ma], axis=0).astype(BF16)
            right = jnp.concatenate([h, m, h, l, h, m], axis=0).astype(BF16)
            step = lax.dot_general(left, right, (((0,), (0,)), ((), ())), preferred_element_type=F32)
            work[low:, :] = work[low:, :] - step[low:, :]


def params(mib):
    return pltpu.CompilerParams(vmem_limit_bytes=mib * 2**20)


def keep_out(x):
    return pltpu.with_memory_space_constraint(x, pltpu.HBM)


def slice_kernel(bases_ref, skeleton_ref, sem):
    source = bases_ref.at[:, pl.ds(bases_ref.shape[1] - RANK, RANK)]
    run_copies([pltpu.make_async_copy(source, skeleton_ref, sem)])


def run_copies(copies):
    for copy in copies:
        copy.start()
    for copy in copies:
        copy.wait()


def find_sibling(own, parent_ref):
    parent = parent_ref[own]

    def step(i, found):
        return jnp.where((parent_ref[i] == parent) & (i != own), i, found)

    return lax.fori_loop(0, parent_ref.shape[0], step, jnp.int32(0), unroll=True)


FIRST, LIVE = 32, 33


def spread_kernel(
    place_ref, index_ref, mask_ref, parent_ref, diag_ref, bases_ref, out_ref, facts_ref, both, sem
):
    rows = diag_ref.shape[0]
    pair = (diag_ref, bases_ref)
    loads = [pltpu.make_async_copy(ref, both.at[pl.ds(q * rows, rows)], sem.at[q]) for q, ref in enumerate(pair)]
    for load in loads:
        load.start()
    own, column = place_ref[0], place_ref[1]
    slots, clusters = index_ref.shape
    half = slots // 2
    for k in range(slots):
        offset = (index_ref[k, own] - own + clusters + half) % clusters
        facts_ref[jnp.where(offset < slots, offset, half)] = k
    for load in loads:
        load.wait()
    stores = [pltpu.make_async_copy(both, out_ref.at[p], sem.at[p]) for p in range(out_ref.shape[0])]
    for store in stores:
        store.start()
    sibling = find_sibling(own, parent_ref)
    facts_ref[FIRST] = (own < sibling).astype(jnp.int32)
    count = slots // out_ref.shape[0]
    for k in range(count):
        slot = column * count + k
        live = mask_ref[0, slot]
        facts_ref[LIVE + 2 * k] = live
        facts_ref[LIVE + 2 * k + 1] = jnp.where(index_ref[slot, own] == sibling, live, 0)
    for store in stores:
        store.wait()


def order_kernel(facts_ref, near0, near1, near3, relay1, relay3, far, out_ref, sem):
    sources = (
        [near0.at[0], near0.at[2], far, near0.at[3]],
        [near1.at[0], near1.at[2], near1.at[1], near1.at[3]],
        [relay1.at[0], relay3.at[0], relay1.at[1], relay3.at[1]],
        [near3.at[0], near3.at[2], near3.at[1], near3.at[3]],
    )
    copies = []
    for d in range(16):
        slot = facts_ref[d]
        target = out_ref.at[slot // 2, slot % 2]
        copies.append(pltpu.make_async_copy(sources[d % 4][d // 4], target, sem.at[d]))
    run_copies(copies)


def factor_kernel(
    column_ref, db_ref, high_ref, low_ref, schur_ref, factor_ref, work, upper1, upper2, full, solve_ref
):
    rows = db_ref.shape[1] // 2
    size = db_ref.shape[0] * rows
    diag = db_ref[:, :rows, :].reshape(size, size)
    basis = db_ref[:, rows:, :].reshape(size, size)
    first = ((0,), (0,))
    red = size - RANK
    reduced = dot_full(dot_full(diag, basis[:, :red]), basis, first)
    skeleton = split2(basis[:, red:])
    corner = dot3(skeleton, split2(dot3(split2(diag), skeleton)), first)
    ri = lax.broadcasted_iota(jnp.int32, (HALF, HALF), 0)
    ci = lax.broadcasted_iota(jnp.int32, (HALF, HALF), 1)
    eye = (ri == ci).astype(F32)
    work[:, :HALF] = reduced[:HALF, :HALF]
    work[:, HALF:] = eye
    factor_half(work, upper1)
    inv1 = upper1[:, HALF:]
    top = dot_full(inv1, reduced[:HALF, HALF:])
    low_t = top[:, :HALF]
    rest = reduced[HALF:red, HALF:] - dot_full(low_t, top, first)
    work[:, :HALF] = rest[:, :HALF]
    work[:, HALF:] = eye
    factor_half(work, upper2)
    inv2 = upper2[:, HALF:]
    couple1 = top[:, HALF:]
    joint = dot_full(inv2, jnp.concatenate([rest[:, HALF:], dot_full(low_t, inv1, first)], axis=1))
    couple2, cross = joint[:, :RANK], joint[:, RANK:]
    solve_ref[:HALF, :] = dot_full(inv1, couple1, first) - dot_full(cross, couple2, first)
    solve_ref[HALF:, :] = dot_full(inv2, couple2, first)
    lift = basis[:, red:] - dot3(split2(basis[:, :red]), split2(solve_ref[...]))
    high_ref[...], low_ref[...] = split2(lift)
    column = column_ref[0]
    count = schur_ref.shape[0]
    start = pl.multiple_of(column * count, count)
    full[...] = corner - (
        dot_full(couple1, couple1, first) + dot_full(couple2, couple2, first)
    )
    schur_ref[...] = full[pl.ds(start, count), :]
    full[:HALF, :HALF] = jnp.where(ri >= ci, upper1[:, :HALF].T, 0.0)
    full[HALF:, :HALF] = low_t.T
    full[:HALF, HALF:] = jnp.zeros((HALF, HALF), F32)
    full[HALF:, HALF:] = jnp.where(ri >= ci, upper2[:, :HALF].T, 0.0)
    factor_ref[...] = full[pl.ds(start, count), :]


def project_kernel(near_ref, high_ref, low_ref, out_high, out_low, block, sem):
    count = near_ref.shape[0]
    loads = [pltpu.make_async_copy(near_ref.at[k], block.at[k], sem.at[k]) for k in range(count)]
    for load in loads:
        load.start()
    lift = high_ref[...], low_ref[...]
    for k in range(count):
        loads[k].wait()
        out_high[k], out_low[k] = split2(dot3(lift, split2(block[k]), ((0,), (0,))))


def slot_product(high_ref, low_ref, routed_ref, k):
    size = high_ref.shape[2]
    partner = routed_ref[:, k].reshape(size, RANK)
    return dot3((high_ref[k], low_ref[k]), split2(partner))


def side_kernel(facts_ref, high_ref, low_ref, routed_ref, side_ref):
    side_ref[...] = jnp.zeros_like(side_ref)
    for k in range(high_ref.shape[0]):

        @pl.when(facts_ref[LIVE + 2 * k + 1] != 0)
        def _():
            side_ref[...] = slot_product(high_ref, low_ref, routed_ref, k).reshape(side_ref.shape)


def couple_kernel(facts_ref, high_ref, low_ref, routed_ref, out_ref):
    for k in range(high_ref.shape[0]):
        live = facts_ref[LIVE + 2 * k].astype(F32)
        out_ref[k] = slot_product(high_ref, low_ref, routed_ref, k) * live


def merge_kernel(facts_ref, parts_ref, schur_ref, out_ref):
    first = facts_ref[FIRST] != 0
    side = parts_ref[0]
    for p in range(1, parts_ref.shape[0]):
        side = side + parts_ref[p]
    schur = schur_ref[...]
    out_ref[:, :RANK] = jnp.where(first, schur, side)
    out_ref[:, RANK:] = jnp.where(first, side, schur)


def shards(near_blocks, diag_block, bases, near_index, near_mask, parent_map):
    columns = lax.axis_size("col")
    clusters = lax.axis_size("clu")
    column = lax.axis_index("col").astype(jnp.int32)
    own = lax.axis_index("clu").astype(jnp.int32)
    place = jnp.stack([own, column])
    rows, size = bases.shape[1:]
    per_device = near_blocks.shape[1]
    shape = jax.ShapeDtypeStruct

    def shift(x, d):
        return lax.ppermute(x, "clu", [((i + d) % clusters, i) for i in range(clusters)])

    skeleton = pl.pallas_call(
        slice_kernel,
        out_shape=shape((rows, RANK), F32),
        in_specs=[HBM],
        out_specs=VMEM,
        scratch_shapes=[pltpu.SemaphoreType.DMA],
        compiler_params=params(4),
        name="skeleton",
    )(keep_out(bases[0]))
    down8 = shift(skeleton, -8)
    far = shift(skeleton, clusters // 2)
    pair = jnp.stack([down8, skeleton])
    up4 = shift(pair, 4)
    spread, facts = pl.pallas_call(
        spread_kernel,
        out_shape=(pltpu.HBM((columns, 2 * rows, size), F32), shape((64,), jnp.int32)),
        in_specs=[SMEM] * 4 + [HBM] * 2,
        out_specs=(HBM, SMEM),
        scratch_shapes=[pltpu.VMEM((2 * rows, size), F32), pltpu.SemaphoreType.DMA((columns,))],
        compiler_params=params(4),
        name="spread",
    )(place, near_index.T, near_mask, parent_map, keep_out(diag_block[0]), keep_out(bases[0]))
    db = lax.all_to_all(spread, "col", split_axis=0, concat_axis=0, tiled=False)
    near0 = jnp.concatenate([pair, up4], axis=0)
    near1 = shift(near0, 1)
    near3 = shift(near0, 3)
    relay1 = shift(near1[:2], 1)
    relay3 = shift(near3[:2], 3)
    ordered = pl.pallas_call(
        order_kernel,
        out_shape=pltpu.HBM((columns, per_device, rows, RANK), F32),
        in_specs=[SMEM] + [ANY] * 6,
        out_specs=HBM,
        compiler_params=params(2),
        scratch_shapes=[pltpu.SemaphoreType.DMA((near_index.shape[1],))],
        name="order",
    )(facts, near0, near1, near3, relay1, relay3, far)
    routed = lax.all_to_all(ordered, "col", split_axis=0, concat_axis=0, tiled=False)
    count = RANK // columns
    high, low, schur, factor = pl.pallas_call(
        factor_kernel,
        out_shape=(
            shape((size, RANK), BF16),
            shape((size, RANK), BF16),
            shape((count, RANK), F32),
            shape(((size - RANK) // columns, size - RANK), F32),
        ),
        in_specs=[SMEM, VMEM],
        out_specs=(VMEM,) * 4,
        scratch_shapes=[pltpu.VMEM((HALF, 2 * HALF), F32)] * 3 + [pltpu.VMEM((RANK, RANK), F32)] * 2,
        cost_estimate=pl.CostEstimate(flops=6_000_000_000, bytes_accessed=4_000_000, transcendentals=0),
        compiler_params=params(24),
        name="factor",
    )(column[None], db)
    projected = (per_device, RANK, size)
    rows_high, rows_low = pl.pallas_call(
        project_kernel,
        out_shape=(shape(projected, BF16),) * 2,
        in_specs=[HBM] + [VMEM] * 2,
        out_specs=(VMEM,) * 2,
        scratch_shapes=[
            pltpu.VMEM(near_blocks.shape[1:], F32),
            pltpu.SemaphoreType.DMA((per_device,)),
        ],
        cost_estimate=pl.CostEstimate(flops=1_000_000_000, bytes_accessed=4_000_000, transcendentals=0),
        compiler_params=params(16),
        name="project",
    )(keep_out(near_blocks[0]), high, low)
    side = pl.pallas_call(
        side_kernel,
        out_shape=shape((columns, count, RANK), F32),
        in_specs=[SMEM] + [VMEM] * 3,
        out_specs=VMEM,
        cost_estimate=pl.CostEstimate(flops=200_000_000, bytes_accessed=2_000_000, transcendentals=0),
        compiler_params=params(8),
        name="side",
    )(facts, rows_high, rows_low, routed)
    parts = lax.all_to_all(side, "col", split_axis=0, concat_axis=0, tiled=False)
    coupling = pl.pallas_call(
        couple_kernel,
        out_shape=shape((per_device, RANK, RANK), F32),
        in_specs=[SMEM] + [VMEM] * 3,
        out_specs=VMEM,
        cost_estimate=pl.CostEstimate(flops=400_000_000, bytes_accessed=4_000_000, transcendentals=0),
        compiler_params=params(8),
        name="couple",
    )(facts, rows_high, rows_low, routed)
    parent_rows = pl.pallas_call(
        merge_kernel,
        out_shape=shape((count, 2 * RANK), F32),
        in_specs=[SMEM] + [VMEM] * 2,
        out_specs=VMEM,
        compiler_params=params(4),
        name="merge",
    )(facts, parts, schur)
    return coupling[None], parent_rows[None], factor[None]


def solution(mesh):
    in_specs = (
        P("clu", "col", None, None),
        P("clu", "col", None),
        P("clu", "col", None),
        P(),
        P("clu", None),
        P(),
    )
    out_specs = (P("clu", "col", None, None), P("clu", "col", None), P("clu", "col", None))
    return jax.shard_map(shards, mesh=mesh, in_specs=in_specs, out_specs=out_specs, check_vma=False)
```

```python
import jax
import jax.numpy as jnp
from jax import lax
from jax.experimental import pallas as pl
from jax.experimental.pallas import tpu as pltpu
from jax.sharding import PartitionSpec as P


RANK = 256
HALF = 128
F32 = jnp.float32
BF16 = jnp.bfloat16
VMEM = pl.BlockSpec(memory_space=pltpu.VMEM)
SMEM = pl.BlockSpec(memory_space=pltpu.SMEM)
ANY = pl.BlockSpec(memory_space=pl.ANY)
HBM = pl.BlockSpec(memory_space=pltpu.HBM)


def dot_full(a, b, dims=((1,), (0,))):
    return lax.dot_general(
        a, b, (dims, ((), ())), precision=lax.Precision.HIGHEST, preferred_element_type=F32
    )


def split2(x):
    high = x.astype(BF16)
    return high, (x - high.astype(F32)).astype(BF16)


def dot3(a, b, dims=((1,), (0,))):
    def one(x, y):
        return lax.dot_general(x, y, (dims, ((), ())), preferred_element_type=F32)

    return one(a[0], b[0]) + (one(a[0], b[1]) + one(a[1], b[0]))


def split3(x):
    high = x.astype(BF16)
    rest = x - high.astype(F32)
    mid = rest.astype(BF16)
    return high, mid, (rest - mid.astype(F32)).astype(BF16)


def factor_half(work, upper):
    sub = lax.broadcasted_iota(jnp.int32, (8, HALF), 0)

    def spread_lane(x, j):
        return jnp.broadcast_to(x[:, j : j + 1], (8, HALF))

    def spread_row(x, m):
        return jnp.broadcast_to(x[m : m + 1, :], (8, HALF))

    rows_a, rows_w = work[0:8, :HALF], work[0:8, HALF:]
    for group in range(HALF // 8):
        base = 8 * group
        columns = [spread_lane(rows_a, base + j) for j in range(8)]
        cell = {(m, j): spread_row(columns[j], m) for j in range(8) for m in range(j, 8)}
        inv = [None] * 8
        ratio = {}
        for k in range(8):
            inv[k] = 1.0 / cell[k, k]
            for m in range(k + 1, 8):
                ratio[m, k] = cell[m, k] * inv[k]
            for j in range(k + 1, 8):
                for m in range(j, 8):
                    cell[m, j] = cell[m, j] - ratio[m, k] * cell[j, k]
        ra = [spread_row(rows_a, m) for m in range(8)]
        rw = [spread_row(rows_w, m) for m in range(8)]
        for m in range(8):
            for k in range(m):
                ra[m] = ra[m] - ratio[m, k] * ra[k]
                rw[m] = rw[m] - ratio[m, k] * rw[k]
        ua = uw = None
        for m in range(8):
            scale = lax.rsqrt(cell[m, m])
            a, w = ra[m] * scale, rw[m] * scale
            ua = a if ua is None else jnp.where(sub == m, a, ua)
            uw = w if uw is None else jnp.where(sub == m, w, uw)
        upper[base : base + 8, :HALF] = ua
        upper[base : base + 8, HALF:] = uw
        after = base + 8
        if after == HALF:
            break
        next_a, next_w = work[after : after + 8, :HALF], work[after : after + 8, HALF:]
        lead = [spread_lane(next_a, base + k) for k in range(8)]
        for k in range(8):
            for j in range(k):
                lead[k] = lead[k] - lead[j] * ratio[k, j]
        for k in range(8):
            factor = lead[k] * inv[k]
            next_a = next_a - factor * ra[k]
            next_w = next_w - factor * rw[k]
        rows_a, rows_w = next_a, next_w
        low = after + 8
        if low < HALF:
            h, m, l = (x.astype(F32) for x in split3(jnp.concatenate([ua, uw], axis=1)))
            ha, ma, la = h[:, :HALF], m[:, :HALF], l[:, :HALF]
            left = jnp.concatenate([ha, ha, ma, ha, la, ma], axis=0).astype(BF16)
            right = jnp.concatenate([h, m, h, l, h, m], axis=0).astype(BF16)
            step = lax.dot_general(left, right, (((0,), (0,)), ((), ())), preferred_element_type=F32)
            work[low:, :] = work[low:, :] - step[low:, :]


def params(mib):
    return pltpu.CompilerParams(vmem_limit_bytes=mib * 2**20)


def keep_out(x):
    return pltpu.with_memory_space_constraint(x, pltpu.HBM)


def slice_kernel(bases_ref, skeleton_ref, sem):
    source = bases_ref.at[:, pl.ds(bases_ref.shape[1] - RANK, RANK)]
    run_copies([pltpu.make_async_copy(source, skeleton_ref, sem)])


def run_copies(copies):
    for copy in copies:
        copy.start()
    for copy in copies:
        copy.wait()


def find_sibling(own, parent_ref):
    parent = parent_ref[own]

    def step(i, found):
        return jnp.where((parent_ref[i] == parent) & (i != own), i, found)

    return lax.fori_loop(0, parent_ref.shape[0], step, jnp.int32(0), unroll=True)


FIRST, LIVE = 32, 33


def spread_kernel(diag_ref, bases_ref, out_ref, both, sem):
    rows = diag_ref.shape[0]
    pair = (diag_ref, bases_ref)
    run_copies(
        [pltpu.make_async_copy(ref, both.at[pl.ds(q * rows, rows)], sem.at[q]) for q, ref in enumerate(pair)]
    )
    run_copies([pltpu.make_async_copy(both, out_ref.at[p], sem.at[p]) for p in range(out_ref.shape[0])])


def facts_kernel(index_ref, mask_ref, parent_ref, facts_ref):
    own, column = lax.axis_index("clu"), lax.axis_index("col")
    slots, clusters = index_ref.shape
    half = slots // 2
    for k in range(slots):
        offset = (index_ref[k, own] - own + clusters + half) % clusters
        facts_ref[jnp.where(offset < slots, offset, half)] = k
    sibling = find_sibling(own, parent_ref)
    facts_ref[FIRST] = (own < sibling).astype(jnp.int32)
    count = slots // lax.axis_size("col")
    for k in range(count):
        slot = column * count + k
        live = mask_ref[0, slot]
        facts_ref[LIVE + 2 * k] = live
        facts_ref[LIVE + 2 * k + 1] = jnp.where(index_ref[slot, own] == sibling, live, 0)


def order_kernel(facts_ref, near0, near1, near2, near3, far, out_ref, sem):
    stacks = (near0, near1, near2, near3)
    copies = []
    for d in range(16):
        slot = facts_ref[d]
        source = far if d == 8 else stacks[d % 4].at[d // 4]
        copies.append(pltpu.make_async_copy(source, out_ref.at[slot // 2, slot % 2], sem.at[d]))
    run_copies(copies)


def factor_kernel(
    db_ref, high_ref, low_ref, schur_ref, factor_ref, work, upper1, upper2, full, solve_ref
):
    rows = db_ref.shape[1] // 2
    size = db_ref.shape[0] * rows
    diag = db_ref[:, :rows, :].reshape(size, size)
    basis = db_ref[:, rows:, :].reshape(size, size)
    first = ((0,), (0,))
    red = size - RANK
    reduced = dot_full(dot_full(diag, basis[:, :red]), basis, first)
    skeleton = split2(basis[:, red:])
    corner = dot3(skeleton, split2(dot3(split2(diag), skeleton)), first)
    ri = lax.broadcasted_iota(jnp.int32, (HALF, HALF), 0)
    ci = lax.broadcasted_iota(jnp.int32, (HALF, HALF), 1)
    eye = (ri == ci).astype(F32)
    work[:, :HALF] = reduced[:HALF, :HALF]
    work[:, HALF:] = eye
    factor_half(work, upper1)
    inv1 = upper1[:, HALF:]
    top = dot_full(inv1, reduced[:HALF, HALF:])
    low_t = top[:, :HALF]
    rest = reduced[HALF:red, HALF:] - dot_full(low_t, top, first)
    work[:, :HALF] = rest[:, :HALF]
    work[:, HALF:] = eye
    factor_half(work, upper2)
    inv2 = upper2[:, HALF:]
    couple1 = top[:, HALF:]
    joint = dot_full(inv2, jnp.concatenate([rest[:, HALF:], dot_full(low_t, inv1, first)], axis=1))
    couple2, cross = joint[:, :RANK], joint[:, RANK:]
    solve_ref[:HALF, :] = dot_full(inv1, couple1, first) - dot_full(cross, couple2, first)
    solve_ref[HALF:, :] = dot_full(inv2, couple2, first)
    lift = basis[:, red:] - dot3(split2(basis[:, :red]), split2(solve_ref[...]))
    high_ref[...], low_ref[...] = split2(lift)
    column = lax.axis_index("col")
    count = schur_ref.shape[0]
    start = pl.multiple_of(column * count, count)
    full[...] = corner - (
        dot_full(couple1, couple1, first) + dot_full(couple2, couple2, first)
    )
    schur_ref[...] = full[pl.ds(start, count), :]
    full[:HALF, :HALF] = jnp.where(ri >= ci, upper1[:, :HALF].T, 0.0)
    full[HALF:, :HALF] = low_t.T
    full[:HALF, HALF:] = jnp.zeros((HALF, HALF), F32)
    full[HALF:, HALF:] = jnp.where(ri >= ci, upper2[:, :HALF].T, 0.0)
    factor_ref[...] = full[pl.ds(start, count), :]


def project_kernel(near_ref, high_ref, low_ref, out_high, out_low, block, sem):
    count = near_ref.shape[0]
    loads = [pltpu.make_async_copy(near_ref.at[k], block.at[k], sem.at[k]) for k in range(count)]
    for load in loads:
        load.start()
    lift = high_ref[...], low_ref[...]
    for k in range(count):
        loads[k].wait()
        out_high[k], out_low[k] = split2(dot3(lift, split2(block[k]), ((0,), (0,))))


def slot_product(high_ref, low_ref, routed_ref, k):
    size = high_ref.shape[2]
    partner = routed_ref[:, k].reshape(size, RANK)
    return dot3((high_ref[k], low_ref[k]), split2(partner))


def side_kernel(facts_ref, high_ref, low_ref, routed_ref, side_ref):
    side_ref[...] = jnp.zeros_like(side_ref)
    for k in range(high_ref.shape[0]):

        @pl.when(facts_ref[LIVE + 2 * k + 1] != 0)
        def _():
            side_ref[...] = slot_product(high_ref, low_ref, routed_ref, k).reshape(side_ref.shape)


def couple_kernel(facts_ref, high_ref, low_ref, routed_ref, out_ref):
    for k in range(high_ref.shape[0]):
        live = facts_ref[LIVE + 2 * k].astype(F32)
        out_ref[k] = slot_product(high_ref, low_ref, routed_ref, k) * live


def merge_kernel(facts_ref, parts_ref, schur_ref, out_ref):
    first = facts_ref[FIRST] != 0
    side = parts_ref[0]
    for p in range(1, parts_ref.shape[0]):
        side = side + parts_ref[p]
    schur = schur_ref[...]
    out_ref[:, :RANK] = jnp.where(first, schur, side)
    out_ref[:, RANK:] = jnp.where(first, side, schur)


def shards(near_blocks, diag_block, bases, near_index, near_mask, parent_map):
    columns = lax.axis_size("col")
    clusters = lax.axis_size("clu")
    rows, size = bases.shape[1:]
    per_device = near_blocks.shape[1]
    shape = jax.ShapeDtypeStruct

    def shift(x, d):
        return lax.ppermute(x, "clu", [((i + d) % clusters, i) for i in range(clusters)])

    skeleton = pl.pallas_call(
        slice_kernel,
        out_shape=shape((rows, RANK), F32),
        in_specs=[HBM],
        out_specs=VMEM,
        scratch_shapes=[pltpu.SemaphoreType.DMA],
        compiler_params=params(4),
        name="skeleton",
    )(keep_out(bases[0]))
    far = shift(skeleton, clusters // 2)
    down8 = shift(skeleton, -8)
    down4 = shift(skeleton, -4)
    up4 = shift(skeleton, 4)
    spread = pl.pallas_call(
        spread_kernel,
        out_shape=pltpu.HBM((columns, 2 * rows, size), F32),
        in_specs=[HBM] * 2,
        out_specs=HBM,
        scratch_shapes=[pltpu.VMEM((2 * rows, size), F32), pltpu.SemaphoreType.DMA((columns,))],
        compiler_params=params(4),
        name="spread",
    )(keep_out(diag_block[0]), keep_out(bases[0]))
    db = lax.all_to_all(spread, "col", split_axis=0, concat_axis=0, tiled=False)
    near0 = jnp.stack([down8, down4, skeleton, up4])
    near2 = shift(near0, 2)
    near1 = shift(near0, 1)
    near3 = shift(near0, 3)
    facts = pl.pallas_call(
        facts_kernel,
        out_shape=shape((64,), jnp.int32),
        in_specs=[SMEM] * 3,
        out_specs=SMEM,
        name="facts",
    )(near_index.T, near_mask, parent_map)
    facts = keep_out(facts)
    ordered = pl.pallas_call(
        order_kernel,
        out_shape=pltpu.HBM((columns, per_device, rows, RANK), F32),
        in_specs=[SMEM] + [ANY] * 5,
        out_specs=HBM,
        compiler_params=params(2),
        scratch_shapes=[pltpu.SemaphoreType.DMA((near_index.shape[1],))],
        name="order",
    )(facts, near0, near1, near2, near3, far)
    routed = lax.all_to_all(ordered, "col", split_axis=0, concat_axis=0, tiled=False)
    count = RANK // columns
    high, low, schur, factor = pl.pallas_call(
        factor_kernel,
        out_shape=(
            shape((size, RANK), BF16),
            shape((size, RANK), BF16),
            shape((count, RANK), F32),
            shape(((size - RANK) // columns, size - RANK), F32),
        ),
        in_specs=[VMEM],
        out_specs=(VMEM,) * 4,
        scratch_shapes=[pltpu.VMEM((HALF, 2 * HALF), F32)] * 3 + [pltpu.VMEM((RANK, RANK), F32)] * 2,
        cost_estimate=pl.CostEstimate(flops=6_000_000_000, bytes_accessed=4_000_000, transcendentals=0),
        compiler_params=params(24),
        name="factor",
    )(db)
    projected = (per_device, RANK, size)
    rows_high, rows_low = pl.pallas_call(
        project_kernel,
        out_shape=(shape(projected, BF16),) * 2,
        in_specs=[HBM] + [VMEM] * 2,
        out_specs=(VMEM,) * 2,
        scratch_shapes=[
            pltpu.VMEM(near_blocks.shape[1:], F32),
            pltpu.SemaphoreType.DMA((per_device,)),
        ],
        cost_estimate=pl.CostEstimate(flops=1_000_000_000, bytes_accessed=4_000_000, transcendentals=0),
        compiler_params=params(16),
        name="project",
    )(keep_out(near_blocks[0]), high, low)
    side = pl.pallas_call(
        side_kernel,
        out_shape=shape((columns, count, RANK), F32),
        in_specs=[SMEM] + [VMEM] * 3,
        out_specs=VMEM,
        cost_estimate=pl.CostEstimate(flops=200_000_000, bytes_accessed=2_000_000, transcendentals=0),
        compiler_params=params(8),
        name="side",
    )(facts, rows_high, rows_low, routed)
    parts = lax.all_to_all(side, "col", split_axis=0, concat_axis=0, tiled=False)
    coupling = pl.pallas_call(
        couple_kernel,
        out_shape=shape((per_device, RANK, RANK), F32),
        in_specs=[SMEM] + [VMEM] * 3,
        out_specs=VMEM,
        cost_estimate=pl.CostEstimate(flops=400_000_000, bytes_accessed=4_000_000, transcendentals=0),
        compiler_params=params(8),
        name="couple",
    )(facts, rows_high, rows_low, routed)
    parent_rows = pl.pallas_call(
        merge_kernel,
        out_shape=shape((count, 2 * RANK), F32),
        in_specs=[SMEM] + [VMEM] * 2,
        out_specs=VMEM,
        compiler_params=params(4),
        name="merge",
    )(facts, parts, schur)
    return coupling[None], parent_rows[None], factor[None]


def solution(mesh):
    in_specs = (
        P("clu", "col", None, None),
        P("clu", "col", None),
        P("clu", "col", None),
        P(),
        P("clu", None),
        P(),
    )
    out_specs = (P("clu", "col", None, None), P("clu", "col", None), P("clu", "col", None))
    return jax.shard_map(shards, mesh=mesh, in_specs=in_specs, out_specs=out_specs, check_vma=False)
```

```python
import jax
import jax.numpy as jnp
from jax import lax
from jax.experimental import pallas as pl
from jax.experimental.pallas import tpu as pltpu
from jax.sharding import PartitionSpec as P


RANK = 256
HALF = 128
F32 = jnp.float32
BF16 = jnp.bfloat16
VMEM = pl.BlockSpec(memory_space=pltpu.VMEM)
SMEM = pl.BlockSpec(memory_space=pltpu.SMEM)
ANY = pl.BlockSpec(memory_space=pl.ANY)
HBM = pl.BlockSpec(memory_space=pltpu.HBM)


def dot_full(a, b, dims=((1,), (0,))):
    return lax.dot_general(
        a, b, (dims, ((), ())), precision=lax.Precision.HIGHEST, preferred_element_type=F32
    )


def split2(x):
    high = x.astype(BF16)
    return high, (x - high.astype(F32)).astype(BF16)


def dot3(a, b, dims=((1,), (0,))):
    def one(x, y):
        return lax.dot_general(x, y, (dims, ((), ())), preferred_element_type=F32)

    return one(a[0], b[0]) + (one(a[0], b[1]) + one(a[1], b[0]))


def split3(x):
    high = x.astype(BF16)
    rest = x - high.astype(F32)
    mid = rest.astype(BF16)
    return high, mid, (rest - mid.astype(F32)).astype(BF16)


def factor_half(work, upper):
    sub = lax.broadcasted_iota(jnp.int32, (8, HALF), 0)

    def spread_lane(x, j):
        return jnp.broadcast_to(x[:, j : j + 1], (8, HALF))

    def spread_row(x, m):
        return jnp.broadcast_to(x[m : m + 1, :], (8, HALF))

    rows_a, rows_w = work[0:8, :HALF], work[0:8, HALF:]
    for group in range(HALF // 8):
        base = 8 * group
        columns = [spread_lane(rows_a, base + j) for j in range(8)]
        cell = {(m, j): spread_row(columns[j], m) for j in range(8) for m in range(j, 8)}
        inv = [None] * 8
        ratio = {}
        for k in range(8):
            inv[k] = 1.0 / cell[k, k]
            for m in range(k + 1, 8):
                ratio[m, k] = cell[m, k] * inv[k]
            for j in range(k + 1, 8):
                for m in range(j, 8):
                    cell[m, j] = cell[m, j] - ratio[m, k] * cell[j, k]
        ra = [spread_row(rows_a, m) for m in range(8)]
        rw = [spread_row(rows_w, m) for m in range(8)]
        for m in range(8):
            for k in range(m):
                ra[m] = ra[m] - ratio[m, k] * ra[k]
                rw[m] = rw[m] - ratio[m, k] * rw[k]
        ua = uw = None
        for m in range(8):
            scale = lax.rsqrt(cell[m, m])
            a, w = ra[m] * scale, rw[m] * scale
            ua = a if ua is None else jnp.where(sub == m, a, ua)
            uw = w if uw is None else jnp.where(sub == m, w, uw)
        upper[base : base + 8, :HALF] = ua
        upper[base : base + 8, HALF:] = uw
        after = base + 8
        if after == HALF:
            break
        next_a, next_w = work[after : after + 8, :HALF], work[after : after + 8, HALF:]
        lead = [spread_lane(next_a, base + k) for k in range(8)]
        for k in range(8):
            for j in range(k):
                lead[k] = lead[k] - lead[j] * ratio[k, j]
        for k in range(8):
            factor = lead[k] * inv[k]
            next_a = next_a - factor * ra[k]
            next_w = next_w - factor * rw[k]
        rows_a, rows_w = next_a, next_w
        low = after + 8
        if low < HALF:
            h, m, l = (x.astype(F32) for x in split3(jnp.concatenate([ua, uw], axis=1)))
            ha, ma, la = h[:, :HALF], m[:, :HALF], l[:, :HALF]
            left = jnp.concatenate([ha, ha, ma, ha, la, ma], axis=0).astype(BF16)
            right = jnp.concatenate([h, m, h, l, h, m], axis=0).astype(BF16)
            step = lax.dot_general(left, right, (((0,), (0,)), ((), ())), preferred_element_type=F32)
            work[low:, :] = work[low:, :] - step[low:, :]


def params(mib):
    return pltpu.CompilerParams(vmem_limit_bytes=mib * 2**20)


def keep_out(x):
    return pltpu.with_memory_space_constraint(x, pltpu.HBM)


def slice_kernel(bases_ref, skeleton_ref, sem):
    source = bases_ref.at[:, pl.ds(bases_ref.shape[1] - RANK, RANK)]
    run_copies([pltpu.make_async_copy(source, skeleton_ref, sem)])


def run_copies(copies):
    for copy in copies:
        copy.start()
    for copy in copies:
        copy.wait()


def find_sibling(own, parent_ref):
    parent = parent_ref[own]

    def step(i, found):
        return jnp.where((parent_ref[i] == parent) & (i != own), i, found)

    return lax.fori_loop(0, parent_ref.shape[0], step, jnp.int32(0), unroll=True)


FIRST, LIVE = 32, 33


def spread_kernel(diag_ref, bases_ref, out_ref, both, sem):
    rows = diag_ref.shape[0]
    pair = (diag_ref, bases_ref)
    run_copies(
        [pltpu.make_async_copy(ref, both.at[pl.ds(q * rows, rows)], sem.at[q]) for q, ref in enumerate(pair)]
    )
    run_copies([pltpu.make_async_copy(both, out_ref.at[p], sem.at[p]) for p in range(out_ref.shape[0])])


def facts_kernel(index_ref, mask_ref, parent_ref, facts_ref):
    own, column = lax.axis_index("clu"), lax.axis_index("col")
    slots, clusters = index_ref.shape
    half = slots // 2
    for k in range(slots):
        offset = (index_ref[k, own] - own + clusters + half) % clusters
        facts_ref[jnp.where(offset < slots, offset, half)] = k
    sibling = find_sibling(own, parent_ref)
    facts_ref[FIRST] = (own < sibling).astype(jnp.int32)
    count = slots // lax.axis_size("col")
    for k in range(count):
        slot = column * count + k
        live = mask_ref[0, slot]
        facts_ref[LIVE + 2 * k] = live
        facts_ref[LIVE + 2 * k + 1] = jnp.where(index_ref[slot, own] == sibling, live, 0)


def order_kernel(facts_ref, near0, near1, near2, relay3, near3, far, out_ref, sem):
    stacks = (near0, near1, near2, near3)
    copies = []
    for d in range(16):
        slot = facts_ref[d]
        if d == 8:
            source = far
        elif d % 4 == 2 and d // 4 >= 2:
            source = relay3.at[d // 4 - 2]
        else:
            source = stacks[d % 4].at[d // 4]
        copies.append(pltpu.make_async_copy(source, out_ref.at[slot // 2, slot % 2], sem.at[d]))
    run_copies(copies)


def factor_kernel(
    mine_ref, theirs_ref, high_ref, low_ref, schur_ref, factor_ref, db_ref, work, upper1, upper2, full, solve_ref
):
    core = lax.axis_index("col") % 2
    for x in range(mine_ref.shape[0]):
        db_ref[2 * x + core] = mine_ref[x]
        db_ref[2 * x + 1 - core] = theirs_ref[x]
    rows = db_ref.shape[1] // 2
    size = db_ref.shape[0] * rows
    diag = db_ref[:, :rows, :].reshape(size, size)
    basis = db_ref[:, rows:, :].reshape(size, size)
    first = ((0,), (0,))
    red = size - RANK
    reduced = dot_full(dot_full(diag, basis[:, :red]), basis, first)
    skeleton = split2(basis[:, red:])
    corner = dot3(skeleton, split2(dot3(split2(diag), skeleton)), first)
    ri = lax.broadcasted_iota(jnp.int32, (HALF, HALF), 0)
    ci = lax.broadcasted_iota(jnp.int32, (HALF, HALF), 1)
    eye = (ri == ci).astype(F32)
    work[:, :HALF] = reduced[:HALF, :HALF]
    work[:, HALF:] = eye
    factor_half(work, upper1)
    inv1 = upper1[:, HALF:]
    top = dot_full(inv1, reduced[:HALF, HALF:])
    low_t = top[:, :HALF]
    rest = reduced[HALF:red, HALF:] - dot_full(low_t, top, first)
    work[:, :HALF] = rest[:, :HALF]
    work[:, HALF:] = eye
    factor_half(work, upper2)
    inv2 = upper2[:, HALF:]
    couple1 = top[:, HALF:]
    joint = dot_full(inv2, jnp.concatenate([rest[:, HALF:], dot_full(low_t, inv1, first)], axis=1))
    couple2, cross = joint[:, :RANK], joint[:, RANK:]
    solve_ref[:HALF, :] = dot_full(inv1, couple1, first) - dot_full(cross, couple2, first)
    solve_ref[HALF:, :] = dot_full(inv2, couple2, first)
    lift = basis[:, red:] - dot3(split2(basis[:, :red]), split2(solve_ref[...]))
    high_ref[...], low_ref[...] = split2(lift)
    column = lax.axis_index("col")
    count = schur_ref.shape[0]
    start = pl.multiple_of(column * count, count)
    full[...] = corner - (
        dot_full(couple1, couple1, first) + dot_full(couple2, couple2, first)
    )
    schur_ref[...] = full[pl.ds(start, count), :]
    full[:HALF, :HALF] = jnp.where(ri >= ci, upper1[:, :HALF].T, 0.0)
    full[HALF:, :HALF] = low_t.T
    full[:HALF, HALF:] = jnp.zeros((HALF, HALF), F32)
    full[HALF:, HALF:] = jnp.where(ri >= ci, upper2[:, :HALF].T, 0.0)
    factor_ref[...] = full[pl.ds(start, count), :]


def project_kernel(near_ref, high_ref, low_ref, out_high, out_low, block, sem):
    count = near_ref.shape[0]
    loads = [pltpu.make_async_copy(near_ref.at[k], block.at[k], sem.at[k]) for k in range(count)]
    for load in loads:
        load.start()
    lift = high_ref[...], low_ref[...]
    for k in range(count):
        loads[k].wait()
        out_high[k], out_low[k] = split2(dot3(lift, split2(block[k]), ((0,), (0,))))


def slot_product(high_ref, low_ref, routed_ref, k):
    size = high_ref.shape[2]
    partner = routed_ref[:, k].reshape(size, RANK)
    return dot3((high_ref[k], low_ref[k]), split2(partner))


def side_kernel(facts_ref, high_ref, low_ref, routed_ref, side_ref):
    side_ref[...] = jnp.zeros_like(side_ref)
    for k in range(high_ref.shape[0]):

        @pl.when(facts_ref[LIVE + 2 * k + 1] != 0)
        def _():
            side_ref[...] = slot_product(high_ref, low_ref, routed_ref, k).reshape(side_ref.shape)


def couple_kernel(facts_ref, high_ref, low_ref, routed_ref, out_ref):
    for k in range(high_ref.shape[0]):
        live = facts_ref[LIVE + 2 * k].astype(F32)
        out_ref[k] = slot_product(high_ref, low_ref, routed_ref, k) * live


def merge_kernel(facts_ref, parts_ref, schur_ref, out_ref):
    first = facts_ref[FIRST] != 0
    side = parts_ref[0]
    for p in range(1, parts_ref.shape[0]):
        side = side + parts_ref[p]
    schur = schur_ref[...]
    out_ref[:, :RANK] = jnp.where(first, schur, side)
    out_ref[:, RANK:] = jnp.where(first, side, schur)


def shards(near_blocks, diag_block, bases, near_index, near_mask, parent_map):
    columns = lax.axis_size("col")
    clusters = lax.axis_size("clu")
    rows, size = bases.shape[1:]
    per_device = near_blocks.shape[1]
    shape = jax.ShapeDtypeStruct

    def shift(x, d):
        return lax.ppermute(x, "clu", [((i + d) % clusters, i) for i in range(clusters)])

    skeleton = pl.pallas_call(
        slice_kernel,
        out_shape=shape((rows, RANK), F32),
        in_specs=[HBM],
        out_specs=VMEM,
        scratch_shapes=[pltpu.SemaphoreType.DMA],
        compiler_params=params(4),
        name="skeleton",
    )(keep_out(bases[0]))
    far = shift(skeleton, clusters // 2)
    down8 = shift(skeleton, -8)
    down4 = shift(skeleton, -4)
    up4 = shift(skeleton, 4)
    chips = columns // 2
    spread = pl.pallas_call(
        spread_kernel,
        out_shape=pltpu.HBM((chips, 2 * rows, size), F32),
        in_specs=[HBM] * 2,
        out_specs=HBM,
        scratch_shapes=[pltpu.VMEM((2 * rows, size), F32), pltpu.SemaphoreType.DMA((chips,))],
        compiler_params=params(4),
        name="spread",
    )(keep_out(diag_block[0]), keep_out(bases[0]))
    same_core = [[2 * x + core for x in range(chips)] for core in range(2)]
    mine = lax.all_to_all(
        spread, "col", split_axis=0, concat_axis=0, axis_index_groups=same_core, tiled=False
    )
    theirs = lax.ppermute(mine, "col", [(c, c ^ 1) for c in range(columns)])
    near0 = jnp.stack([down8, down4, skeleton, up4])
    near2 = shift(jnp.stack([down8, down4]), 2)
    near1 = shift(near0, 1)
    near3 = shift(near0, 3)
    relay3 = shift(near3[1:3], 3)
    facts = pl.pallas_call(
        facts_kernel,
        out_shape=shape((64,), jnp.int32),
        in_specs=[SMEM] * 3,
        out_specs=SMEM,
        name="facts",
    )(near_index.T, near_mask, parent_map)
    facts = keep_out(facts)
    ordered = pl.pallas_call(
        order_kernel,
        out_shape=pltpu.HBM((columns, per_device, rows, RANK), F32),
        in_specs=[SMEM] + [ANY] * 6,
        out_specs=HBM,
        compiler_params=params(2),
        scratch_shapes=[pltpu.SemaphoreType.DMA((near_index.shape[1],))],
        name="order",
    )(facts, near0, near1, near2, relay3, near3, far)
    routed = lax.all_to_all(ordered, "col", split_axis=0, concat_axis=0, tiled=False)
    count = RANK // columns
    high, low, schur, factor = pl.pallas_call(
        factor_kernel,
        out_shape=(
            shape((size, RANK), BF16),
            shape((size, RANK), BF16),
            shape((count, RANK), F32),
            shape(((size - RANK) // columns, size - RANK), F32),
        ),
        in_specs=[VMEM] * 2,
        out_specs=(VMEM,) * 4,
        scratch_shapes=[pltpu.VMEM((columns, 2 * rows, size), F32)]
        + [pltpu.VMEM((HALF, 2 * HALF), F32)] * 3
        + [pltpu.VMEM((RANK, RANK), F32)] * 2,
        cost_estimate=pl.CostEstimate(flops=6_000_000_000, bytes_accessed=4_000_000, transcendentals=0),
        compiler_params=params(24),
        name="factor",
    )(mine, theirs)
    projected = (per_device, RANK, size)
    rows_high, rows_low = pl.pallas_call(
        project_kernel,
        out_shape=(shape(projected, BF16),) * 2,
        in_specs=[HBM] + [VMEM] * 2,
        out_specs=(VMEM,) * 2,
        scratch_shapes=[
            pltpu.VMEM(near_blocks.shape[1:], F32),
            pltpu.SemaphoreType.DMA((per_device,)),
        ],
        cost_estimate=pl.CostEstimate(flops=1_000_000_000, bytes_accessed=4_000_000, transcendentals=0),
        compiler_params=params(16),
        name="project",
    )(keep_out(near_blocks[0]), high, low)
    side = pl.pallas_call(
        side_kernel,
        out_shape=shape((columns, count, RANK), F32),
        in_specs=[SMEM] + [VMEM] * 3,
        out_specs=VMEM,
        cost_estimate=pl.CostEstimate(flops=200_000_000, bytes_accessed=2_000_000, transcendentals=0),
        compiler_params=params(8),
        name="side",
    )(facts, rows_high, rows_low, routed)
    parts = lax.all_to_all(side, "col", split_axis=0, concat_axis=0, tiled=False)
    coupling = pl.pallas_call(
        couple_kernel,
        out_shape=shape((per_device, RANK, RANK), F32),
        in_specs=[SMEM] + [VMEM] * 3,
        out_specs=VMEM,
        cost_estimate=pl.CostEstimate(flops=400_000_000, bytes_accessed=4_000_000, transcendentals=0),
        compiler_params=params(8),
        name="couple",
    )(facts, rows_high, rows_low, routed)
    parent_rows = pl.pallas_call(
        merge_kernel,
        out_shape=shape((count, 2 * RANK), F32),
        in_specs=[SMEM] + [VMEM] * 2,
        out_specs=VMEM,
        compiler_params=params(4),
        name="merge",
    )(facts, parts, schur)
    return coupling[None], parent_rows[None], factor[None]


def solution(mesh):
    in_specs = (
        P("clu", "col", None, None),
        P("clu", "col", None),
        P("clu", "col", None),
        P(),
        P("clu", None),
        P(),
    )
    out_specs = (P("clu", "col", None, None), P("clu", "col", None), P("clu", "col", None))
    return jax.shard_map(shards, mesh=mesh, in_specs=in_specs, out_specs=out_specs, check_vma=False)
```

```python
import jax
import jax.numpy as jnp
from jax import lax
from jax.experimental import pallas as pl
from jax.experimental.pallas import tpu as pltpu
from jax.sharding import PartitionSpec as P


RANK = 256
HALF = 128
F32 = jnp.float32
BF16 = jnp.bfloat16
VMEM = pl.BlockSpec(memory_space=pltpu.VMEM)
SMEM = pl.BlockSpec(memory_space=pltpu.SMEM)
ANY = pl.BlockSpec(memory_space=pl.ANY)
HBM = pl.BlockSpec(memory_space=pltpu.HBM)


def dot_full(a, b, dims=((1,), (0,))):
    return lax.dot_general(
        a, b, (dims, ((), ())), precision=lax.Precision.HIGHEST, preferred_element_type=F32
    )


def split2(x):
    high = x.astype(BF16)
    return high, (x - high.astype(F32)).astype(BF16)


def dot3(a, b, dims=((1,), (0,))):
    def one(x, y):
        return lax.dot_general(x, y, (dims, ((), ())), preferred_element_type=F32)

    return one(a[0], b[0]) + (one(a[0], b[1]) + one(a[1], b[0]))


def split3(x):
    high = x.astype(BF16)
    rest = x - high.astype(F32)
    mid = rest.astype(BF16)
    return high, mid, (rest - mid.astype(F32)).astype(BF16)


def factor_half(work, upper):
    sub = lax.broadcasted_iota(jnp.int32, (8, HALF), 0)

    def spread_lane(x, j):
        return jnp.broadcast_to(x[:, j : j + 1], (8, HALF))

    def spread_row(x, m):
        return jnp.broadcast_to(x[m : m + 1, :], (8, HALF))

    rows_a, rows_w = work[0:8, :HALF], work[0:8, HALF:]
    for group in range(HALF // 8):
        base = 8 * group
        columns = [spread_lane(rows_a, base + j) for j in range(8)]
        cell = {(m, j): spread_row(columns[j], m) for j in range(8) for m in range(j, 8)}
        inv = [None] * 8
        ratio = {}
        for k in range(8):
            inv[k] = 1.0 / cell[k, k]
            for m in range(k + 1, 8):
                ratio[m, k] = cell[m, k] * inv[k]
            for j in range(k + 1, 8):
                for m in range(j, 8):
                    cell[m, j] = cell[m, j] - ratio[m, k] * cell[j, k]
        ra = [spread_row(rows_a, m) for m in range(8)]
        rw = [spread_row(rows_w, m) for m in range(8)]
        for m in range(8):
            for k in range(m):
                ra[m] = ra[m] - ratio[m, k] * ra[k]
                rw[m] = rw[m] - ratio[m, k] * rw[k]
        ua = uw = None
        for m in range(8):
            scale = lax.rsqrt(cell[m, m])
            a, w = ra[m] * scale, rw[m] * scale
            ua = a if ua is None else jnp.where(sub == m, a, ua)
            uw = w if uw is None else jnp.where(sub == m, w, uw)
        upper[base : base + 8, :HALF] = ua
        upper[base : base + 8, HALF:] = uw
        after = base + 8
        if after == HALF:
            break
        next_a, next_w = work[after : after + 8, :HALF], work[after : after + 8, HALF:]
        lead = [spread_lane(next_a, base + k) for k in range(8)]
        for k in range(8):
            for j in range(k):
                lead[k] = lead[k] - lead[j] * ratio[k, j]
        for k in range(8):
            factor = lead[k] * inv[k]
            next_a = next_a - factor * ra[k]
            next_w = next_w - factor * rw[k]
        rows_a, rows_w = next_a, next_w
        low = after + 8
        if low < HALF:
            h, m, l = (x.astype(F32) for x in split3(jnp.concatenate([ua, uw], axis=1)))
            ha, ma, la = h[:, :HALF], m[:, :HALF], l[:, :HALF]
            left = jnp.concatenate([ha, ha, ma, ha, la, ma], axis=0).astype(BF16)
            right = jnp.concatenate([h, m, h, l, h, m], axis=0).astype(BF16)
            step = lax.dot_general(left, right, (((0,), (0,)), ((), ())), preferred_element_type=F32)
            work[low:, :] = work[low:, :] - step[low:, :]


def params(mib):
    return pltpu.CompilerParams(vmem_limit_bytes=mib * 2**20)


def keep_out(x):
    return pltpu.with_memory_space_constraint(x, pltpu.HBM)


def slice_kernel(bases_ref, skeleton_ref, sem):
    source = bases_ref.at[:, pl.ds(bases_ref.shape[1] - RANK, RANK)]
    run_copies([pltpu.make_async_copy(source, skeleton_ref, sem)])


def run_copies(copies):
    for copy in copies:
        copy.start()
    for copy in copies:
        copy.wait()


def find_sibling(own, parent_ref):
    parent = parent_ref[own]

    def step(i, found):
        return jnp.where((parent_ref[i] == parent) & (i != own), i, found)

    return lax.fori_loop(0, parent_ref.shape[0], step, jnp.int32(0), unroll=True)


FIRST, LIVE = 32, 33


def spread_kernel(diag_ref, bases_ref, out_ref, both, sem):
    rows = diag_ref.shape[0]
    pair = (diag_ref, bases_ref)
    run_copies(
        [pltpu.make_async_copy(ref, both.at[pl.ds(q * rows, rows)], sem.at[q]) for q, ref in enumerate(pair)]
    )
    run_copies([pltpu.make_async_copy(both, out_ref.at[p], sem.at[p]) for p in range(out_ref.shape[0])])


def facts_kernel(index_ref, mask_ref, parent_ref, facts_ref):
    own, column = lax.axis_index("clu"), lax.axis_index("col")
    slots, clusters = index_ref.shape
    half = slots // 2
    for k in range(slots):
        offset = (index_ref[k, own] - own + clusters + half) % clusters
        facts_ref[jnp.where(offset < slots, offset, half)] = k
    sibling = find_sibling(own, parent_ref)
    facts_ref[FIRST] = (own < sibling).astype(jnp.int32)
    count = slots // lax.axis_size("col")
    for k in range(count):
        slot = column * count + k
        live = mask_ref[0, slot]
        facts_ref[LIVE + 2 * k] = live
        facts_ref[LIVE + 2 * k + 1] = jnp.where(index_ref[slot, own] == sibling, live, 0)


RING = 4


def fan_kernel(down8, down4, own, up4, up8, out1, out2, out3, sem):
    place = lax.axis_index("clu") % RING
    pieces = (down8, down4, own, up4, up8)
    outs = (out1, out2, out3)
    for r, out in enumerate(outs, 1):
        for wraps in (0, 1):

            @pl.when((place < r) if wraps else (place >= r))
            def _():
                for q in range(RING):
                    pltpu.make_async_copy(pieces[q + wraps], out.at[q], sem.at[r - 1, q]).start()

    for r, out in enumerate(outs, 1):
        for q in range(RING):
            pltpu.make_async_copy(pieces[q], out.at[q], sem.at[r - 1, q]).wait()


def order_kernel(facts_ref, down8, down4, up4, near1, near2, near3, far, out_ref, sem):
    own = (down8, down4, None, up4)
    stacks = (None, near1, near2, near3)
    copies = []
    for d in range(16):
        slot = facts_ref[d]
        if d % 4 == 0:
            source = far if d == 8 else own[d // 4]
        else:
            source = stacks[d % 4].at[d // 4]
        copies.append(pltpu.make_async_copy(source, out_ref.at[slot // 2, slot % 2], sem.at[d]))
    run_copies(copies)


def factor_kernel(
    mine_ref, theirs_ref, high_ref, low_ref, schur_ref, factor_ref, db_ref, work, upper1, upper2, full, solve_ref
):
    core = lax.axis_index("col") % 2
    for x in range(mine_ref.shape[0]):
        db_ref[2 * x + core] = mine_ref[x]
        db_ref[2 * x + 1 - core] = theirs_ref[x]
    rows = db_ref.shape[1] // 2
    size = db_ref.shape[0] * rows
    diag = db_ref[:, :rows, :].reshape(size, size)
    basis = db_ref[:, rows:, :].reshape(size, size)
    first = ((0,), (0,))
    red = size - RANK
    reduced = dot_full(dot_full(diag, basis[:, :red]), basis, first)
    skeleton = split2(basis[:, red:])
    corner = dot3(skeleton, split2(dot3(split2(diag), skeleton)), first)
    ri = lax.broadcasted_iota(jnp.int32, (HALF, HALF), 0)
    ci = lax.broadcasted_iota(jnp.int32, (HALF, HALF), 1)
    eye = (ri == ci).astype(F32)
    work[:, :HALF] = reduced[:HALF, :HALF]
    work[:, HALF:] = eye
    factor_half(work, upper1)
    inv1 = upper1[:, HALF:]
    top = dot_full(inv1, reduced[:HALF, HALF:])
    low_t = top[:, :HALF]
    rest = reduced[HALF:red, HALF:] - dot_full(low_t, top, first)
    work[:, :HALF] = rest[:, :HALF]
    work[:, HALF:] = eye
    factor_half(work, upper2)
    inv2 = upper2[:, HALF:]
    couple1 = top[:, HALF:]
    joint = dot_full(inv2, jnp.concatenate([rest[:, HALF:], dot_full(low_t, inv1, first)], axis=1))
    couple2, cross = joint[:, :RANK], joint[:, RANK:]
    solve_ref[:HALF, :] = dot_full(inv1, couple1, first) - dot_full(cross, couple2, first)
    solve_ref[HALF:, :] = dot_full(inv2, couple2, first)
    lift = basis[:, red:] - dot3(split2(basis[:, :red]), split2(solve_ref[...]))
    high_ref[...], low_ref[...] = split2(lift)
    column = lax.axis_index("col")
    count = schur_ref.shape[0]
    start = pl.multiple_of(column * count, count)
    full[...] = corner - (
        dot_full(couple1, couple1, first) + dot_full(couple2, couple2, first)
    )
    schur_ref[...] = full[pl.ds(start, count), :]
    full[:HALF, :HALF] = jnp.where(ri >= ci, upper1[:, :HALF].T, 0.0)
    full[HALF:, :HALF] = low_t.T
    full[:HALF, HALF:] = jnp.zeros((HALF, HALF), F32)
    full[HALF:, HALF:] = jnp.where(ri >= ci, upper2[:, :HALF].T, 0.0)
    factor_ref[...] = full[pl.ds(start, count), :]


def project_kernel(near_ref, high_ref, low_ref, out_high, out_low, block, sem):
    count = near_ref.shape[0]
    loads = [pltpu.make_async_copy(near_ref.at[k], block.at[k], sem.at[k]) for k in range(count)]
    for load in loads:
        load.start()
    lift = high_ref[...], low_ref[...]
    for k in range(count):
        loads[k].wait()
        out_high[k], out_low[k] = split2(dot3(lift, split2(block[k]), ((0,), (0,))))


def slot_product(high_ref, low_ref, routed_ref, k):
    size = high_ref.shape[2]
    partner = routed_ref[:, k].reshape(size, RANK)
    return dot3((high_ref[k], low_ref[k]), split2(partner))


def side_kernel(facts_ref, high_ref, low_ref, routed_ref, side_ref):
    side_ref[...] = jnp.zeros_like(side_ref)
    for k in range(high_ref.shape[0]):

        @pl.when(facts_ref[LIVE + 2 * k + 1] != 0)
        def _():
            side_ref[...] = slot_product(high_ref, low_ref, routed_ref, k).reshape(side_ref.shape)


def couple_kernel(facts_ref, high_ref, low_ref, routed_ref, out_ref):
    for k in range(high_ref.shape[0]):
        live = facts_ref[LIVE + 2 * k].astype(F32)
        out_ref[k] = slot_product(high_ref, low_ref, routed_ref, k) * live


def merge_kernel(facts_ref, parts_ref, schur_ref, out_ref):
    first = facts_ref[FIRST] != 0
    side = parts_ref[0]
    for p in range(1, parts_ref.shape[0]):
        side = side + parts_ref[p]
    schur = schur_ref[...]
    out_ref[:, :RANK] = jnp.where(first, schur, side)
    out_ref[:, RANK:] = jnp.where(first, side, schur)


def shards(near_blocks, diag_block, bases, near_index, near_mask, parent_map):
    columns = lax.axis_size("col")
    clusters = lax.axis_size("clu")
    rows, size = bases.shape[1:]
    per_device = near_blocks.shape[1]
    shape = jax.ShapeDtypeStruct

    def shift(x, d):
        return lax.ppermute(x, "clu", [((i + d) % clusters, i) for i in range(clusters)])

    def shift_ring(x, r):
        pairs = [(i - i % RING + (i + r) % RING, i) for i in range(clusters)]
        return lax.ppermute(x, "clu", pairs)

    skeleton = pl.pallas_call(
        slice_kernel,
        out_shape=shape((rows, RANK), F32),
        in_specs=[HBM],
        out_specs=VMEM,
        scratch_shapes=[pltpu.SemaphoreType.DMA],
        compiler_params=params(4),
        name="skeleton",
    )(keep_out(bases[0]))
    far = shift(skeleton, clusters // 2)
    down8 = shift(skeleton, -8)
    up8 = shift(skeleton, 8)
    down4 = shift(skeleton, -4)
    up4 = shift(skeleton, 4)
    chips = columns // 2
    spread = pl.pallas_call(
        spread_kernel,
        out_shape=pltpu.HBM((chips, 2 * rows, size), F32),
        in_specs=[HBM] * 2,
        out_specs=HBM,
        scratch_shapes=[pltpu.VMEM((2 * rows, size), F32), pltpu.SemaphoreType.DMA((chips,))],
        compiler_params=params(4),
        name="spread",
    )(keep_out(diag_block[0]), keep_out(bases[0]))
    same_core = [[2 * x + core for x in range(chips)] for core in range(2)]
    mine = lax.all_to_all(
        spread, "col", split_axis=0, concat_axis=0, axis_index_groups=same_core, tiled=False
    )
    theirs = lax.ppermute(mine, "col", [(c, c ^ 1) for c in range(columns)])
    fan = pl.pallas_call(
        fan_kernel,
        out_shape=(shape((RING, rows, RANK), F32),) * 3,
        in_specs=[ANY] * 5,
        out_specs=(ANY,) * 3,
        scratch_shapes=[pltpu.SemaphoreType.DMA((3, RING))],
        compiler_params=params(2),
        name="fan",
    )(down8, down4, skeleton, up4, up8)
    near2 = shift_ring(fan[1], 2)
    near1 = shift_ring(fan[0], 1)
    near3 = shift_ring(fan[2], 3)
    facts = pl.pallas_call(
        facts_kernel,
        out_shape=shape((64,), jnp.int32),
        in_specs=[SMEM] * 3,
        out_specs=SMEM,
        name="facts",
    )(near_index.T, near_mask, parent_map)
    facts = keep_out(facts)
    ordered = pl.pallas_call(
        order_kernel,
        out_shape=pltpu.HBM((columns, per_device, rows, RANK), F32),
        in_specs=[SMEM] + [ANY] * 7,
        out_specs=HBM,
        compiler_params=params(2),
        scratch_shapes=[pltpu.SemaphoreType.DMA((near_index.shape[1],))],
        name="order",
    )(facts, down8, down4, up4, near1, near2, near3, far)
    routed = lax.all_to_all(ordered, "col", split_axis=0, concat_axis=0, tiled=False)
    count = RANK // columns
    high, low, schur, factor = pl.pallas_call(
        factor_kernel,
        out_shape=(
            shape((size, RANK), BF16),
            shape((size, RANK), BF16),
            shape((count, RANK), F32),
            shape(((size - RANK) // columns, size - RANK), F32),
        ),
        in_specs=[VMEM] * 2,
        out_specs=(VMEM,) * 4,
        scratch_shapes=[pltpu.VMEM((columns, 2 * rows, size), F32)]
        + [pltpu.VMEM((HALF, 2 * HALF), F32)] * 3
        + [pltpu.VMEM((RANK, RANK), F32)] * 2,
        cost_estimate=pl.CostEstimate(flops=6_000_000_000, bytes_accessed=4_000_000, transcendentals=0),
        compiler_params=params(24),
        name="factor",
    )(mine, theirs)
    projected = (per_device, RANK, size)
    rows_high, rows_low = pl.pallas_call(
        project_kernel,
        out_shape=(shape(projected, BF16),) * 2,
        in_specs=[HBM] + [VMEM] * 2,
        out_specs=(VMEM,) * 2,
        scratch_shapes=[
            pltpu.VMEM(near_blocks.shape[1:], F32),
            pltpu.SemaphoreType.DMA((per_device,)),
        ],
        cost_estimate=pl.CostEstimate(flops=1_000_000_000, bytes_accessed=4_000_000, transcendentals=0),
        compiler_params=params(16),
        name="project",
    )(keep_out(near_blocks[0]), high, low)
    side = pl.pallas_call(
        side_kernel,
        out_shape=shape((columns, count, RANK), F32),
        in_specs=[SMEM] + [VMEM] * 3,
        out_specs=VMEM,
        cost_estimate=pl.CostEstimate(flops=200_000_000, bytes_accessed=2_000_000, transcendentals=0),
        compiler_params=params(8),
        name="side",
    )(facts, rows_high, rows_low, routed)
    parts = lax.all_to_all(side, "col", split_axis=0, concat_axis=0, tiled=False)
    coupling = pl.pallas_call(
        couple_kernel,
        out_shape=shape((per_device, RANK, RANK), F32),
        in_specs=[SMEM] + [VMEM] * 3,
        out_specs=VMEM,
        cost_estimate=pl.CostEstimate(flops=400_000_000, bytes_accessed=4_000_000, transcendentals=0),
        compiler_params=params(8),
        name="couple",
    )(facts, rows_high, rows_low, routed)
    parent_rows = pl.pallas_call(
        merge_kernel,
        out_shape=shape((count, 2 * RANK), F32),
        in_specs=[SMEM] + [VMEM] * 2,
        out_specs=VMEM,
        compiler_params=params(4),
        name="merge",
    )(facts, parts, schur)
    return coupling[None], parent_rows[None], factor[None]


def solution(mesh):
    in_specs = (
        P("clu", "col", None, None),
        P("clu", "col", None),
        P("clu", "col", None),
        P(),
        P("clu", None),
        P(),
    )
    out_specs = (P("clu", "col", None, None), P("clu", "col", None), P("clu", "col", None))
    return jax.shard_map(shards, mesh=mesh, in_specs=in_specs, out_specs=out_specs, check_vma=False)
```

```python
import jax
import jax.numpy as jnp
from jax import lax
from jax.experimental import pallas as pl
from jax.experimental.pallas import tpu as pltpu
from jax.sharding import PartitionSpec as P


RANK = 256
HALF = 128
F32 = jnp.float32
BF16 = jnp.bfloat16
VMEM = pl.BlockSpec(memory_space=pltpu.VMEM)
SMEM = pl.BlockSpec(memory_space=pltpu.SMEM)
ANY = pl.BlockSpec(memory_space=pl.ANY)
HBM = pl.BlockSpec(memory_space=pltpu.HBM)


def dot_full(a, b, dims=((1,), (0,))):
    return lax.dot_general(
        a, b, (dims, ((), ())), precision=lax.Precision.HIGHEST, preferred_element_type=F32
    )


def split2(x):
    high = x.astype(BF16)
    return high, (x - high.astype(F32)).astype(BF16)


def dot3(a, b, dims=((1,), (0,))):
    def one(x, y):
        return lax.dot_general(x, y, (dims, ((), ())), preferred_element_type=F32)

    return one(a[0], b[0]) + (one(a[0], b[1]) + one(a[1], b[0]))


def split3(x):
    high = x.astype(BF16)
    rest = x - high.astype(F32)
    mid = rest.astype(BF16)
    return high, mid, (rest - mid.astype(F32)).astype(BF16)


def factor_half(work, upper):
    sub = lax.broadcasted_iota(jnp.int32, (8, HALF), 0)

    def spread_lane(x, j):
        return jnp.broadcast_to(x[:, j : j + 1], (8, HALF))

    def spread_row(x, m):
        return jnp.broadcast_to(x[m : m + 1, :], (8, HALF))

    rows_a, rows_w = work[0:8, :HALF], work[0:8, HALF:]
    for group in range(HALF // 8):
        base = 8 * group
        columns = [spread_lane(rows_a, base + j) for j in range(8)]
        cell = {(m, j): spread_row(columns[j], m) for j in range(8) for m in range(j, 8)}
        inv = [None] * 8
        ratio = {}
        for k in range(8):
            inv[k] = 1.0 / cell[k, k]
            for m in range(k + 1, 8):
                ratio[m, k] = cell[m, k] * inv[k]
            for j in range(k + 1, 8):
                for m in range(j, 8):
                    cell[m, j] = cell[m, j] - ratio[m, k] * cell[j, k]
        ra = [spread_row(rows_a, m) for m in range(8)]
        rw = [spread_row(rows_w, m) for m in range(8)]
        for m in range(8):
            for k in range(m):
                ra[m] = ra[m] - ratio[m, k] * ra[k]
                rw[m] = rw[m] - ratio[m, k] * rw[k]
        ua = uw = None
        for m in range(8):
            scale = lax.rsqrt(cell[m, m])
            a, w = ra[m] * scale, rw[m] * scale
            ua = a if ua is None else jnp.where(sub == m, a, ua)
            uw = w if uw is None else jnp.where(sub == m, w, uw)
        upper[base : base + 8, :HALF] = ua
        upper[base : base + 8, HALF:] = uw
        after = base + 8
        if after == HALF:
            break
        next_a, next_w = work[after : after + 8, :HALF], work[after : after + 8, HALF:]
        lead = [spread_lane(next_a, base + k) for k in range(8)]
        for k in range(8):
            for j in range(k):
                lead[k] = lead[k] - lead[j] * ratio[k, j]
        for k in range(8):
            factor = lead[k] * inv[k]
            next_a = next_a - factor * ra[k]
            next_w = next_w - factor * rw[k]
        rows_a, rows_w = next_a, next_w
        low = after + 8
        if low < HALF:
            h, m, l = (x.astype(F32) for x in split3(jnp.concatenate([ua, uw], axis=1)))
            ha, ma, la = h[:, :HALF], m[:, :HALF], l[:, :HALF]
            left = jnp.concatenate([ha, ha, ma, ha, la, ma], axis=0).astype(BF16)
            right = jnp.concatenate([h, m, h, l, h, m], axis=0).astype(BF16)
            step = lax.dot_general(left, right, (((0,), (0,)), ((), ())), preferred_element_type=F32)
            work[low:, :] = work[low:, :] - step[low:, :]


def params(mib):
    return pltpu.CompilerParams(vmem_limit_bytes=mib * 2**20)


def keep_out(x):
    return pltpu.with_memory_space_constraint(x, pltpu.HBM)


def slice_kernel(bases_ref, skeleton_ref, sem):
    source = bases_ref.at[:, pl.ds(bases_ref.shape[1] - RANK, RANK)]
    run_copies([pltpu.make_async_copy(source, skeleton_ref, sem)])


def run_copies(copies):
    for copy in copies:
        copy.start()
    for copy in copies:
        copy.wait()


def find_sibling(own, parent_ref):
    parent = parent_ref[own]

    def step(i, found):
        return jnp.where((parent_ref[i] == parent) & (i != own), i, found)

    return lax.fori_loop(0, parent_ref.shape[0], step, jnp.int32(0), unroll=True)


FIRST, LIVE = 32, 33


def spread_kernel(diag_ref, bases_ref, out_ref, both, sem):
    rows = diag_ref.shape[0]
    pair = (diag_ref, bases_ref)
    run_copies(
        [pltpu.make_async_copy(ref, both.at[pl.ds(q * rows, rows)], sem.at[q]) for q, ref in enumerate(pair)]
    )
    run_copies([pltpu.make_async_copy(both, out_ref.at[p], sem.at[p]) for p in range(out_ref.shape[0])])


def facts_kernel(index_ref, mask_ref, parent_ref, facts_ref):
    own, column = lax.axis_index("clu"), lax.axis_index("col")
    slots, clusters = index_ref.shape
    half = slots // 2
    for k in range(slots):
        offset = (index_ref[k, own] - own + clusters + half) % clusters
        facts_ref[jnp.where(offset < slots, offset, half)] = k
    sibling = find_sibling(own, parent_ref)
    facts_ref[FIRST] = (own < sibling).astype(jnp.int32)
    count = slots // lax.axis_size("col")
    for k in range(count):
        slot = column * count + k
        live = mask_ref[0, slot]
        facts_ref[LIVE + 2 * k] = live
        facts_ref[LIVE + 2 * k + 1] = jnp.where(index_ref[slot, own] == sibling, live, 0)


def order_kernel(facts_ref, near0, near1, near2, near3, far, out_ref, sem):
    stacks = (near0, near1, near2, near3)
    copies = []
    for d in range(16):
        slot = facts_ref[d]
        source = far if d == 8 else stacks[d % 4].at[d // 4]
        copies.append(pltpu.make_async_copy(source, out_ref.at[slot // 2, slot % 2], sem.at[d]))
    run_copies(copies)


def factor_kernel(
    mine_ref, theirs_ref, high_ref, low_ref, schur_ref, factor_ref, db_ref, work, upper1, upper2, full, solve_ref
):
    core = lax.axis_index("col") % 2
    for x in range(mine_ref.shape[0]):
        db_ref[2 * x + core] = mine_ref[x]
        db_ref[2 * x + 1 - core] = theirs_ref[x]
    rows = db_ref.shape[1] // 2
    size = db_ref.shape[0] * rows
    diag = db_ref[:, :rows, :].reshape(size, size)
    basis = db_ref[:, rows:, :].reshape(size, size)
    first = ((0,), (0,))
    red = size - RANK
    reduced = dot_full(dot_full(diag, basis[:, :red]), basis, first)
    skeleton = split2(basis[:, red:])
    corner = dot3(skeleton, split2(dot3(split2(diag), skeleton)), first)
    ri = lax.broadcasted_iota(jnp.int32, (HALF, HALF), 0)
    ci = lax.broadcasted_iota(jnp.int32, (HALF, HALF), 1)
    eye = (ri == ci).astype(F32)
    work[:, :HALF] = reduced[:HALF, :HALF]
    work[:, HALF:] = eye
    factor_half(work, upper1)
    inv1 = upper1[:, HALF:]
    top = dot_full(inv1, reduced[:HALF, HALF:])
    low_t = top[:, :HALF]
    rest = reduced[HALF:red, HALF:] - dot_full(low_t, top, first)
    work[:, :HALF] = rest[:, :HALF]
    work[:, HALF:] = eye
    factor_half(work, upper2)
    inv2 = upper2[:, HALF:]
    couple1 = top[:, HALF:]
    joint = dot_full(inv2, jnp.concatenate([rest[:, HALF:], dot_full(low_t, inv1, first)], axis=1))
    couple2, cross = joint[:, :RANK], joint[:, RANK:]
    solve_ref[:HALF, :] = dot_full(inv1, couple1, first) - dot_full(cross, couple2, first)
    solve_ref[HALF:, :] = dot_full(inv2, couple2, first)
    lift = basis[:, red:] - dot3(split2(basis[:, :red]), split2(solve_ref[...]))
    high_ref[...], low_ref[...] = split2(lift)
    column = lax.axis_index("col")
    count = schur_ref.shape[0]
    start = pl.multiple_of(column * count, count)
    full[...] = corner - (
        dot_full(couple1, couple1, first) + dot_full(couple2, couple2, first)
    )
    schur_ref[...] = full[pl.ds(start, count), :]
    full[:HALF, :HALF] = jnp.where(ri >= ci, upper1[:, :HALF].T, 0.0)
    full[HALF:, :HALF] = low_t.T
    full[:HALF, HALF:] = jnp.zeros((HALF, HALF), F32)
    full[HALF:, HALF:] = jnp.where(ri >= ci, upper2[:, :HALF].T, 0.0)
    factor_ref[...] = full[pl.ds(start, count), :]


def project_kernel(near_ref, high_ref, low_ref, out_high, out_low, block, sem):
    count = near_ref.shape[0]
    loads = [pltpu.make_async_copy(near_ref.at[k], block.at[k], sem.at[k]) for k in range(count)]
    for load in loads:
        load.start()
    lift = high_ref[...], low_ref[...]
    for k in range(count):
        loads[k].wait()
        out_high[k], out_low[k] = split2(dot3(lift, split2(block[k]), ((0,), (0,))))


def slot_product(high_ref, low_ref, routed_ref, k):
    size = high_ref.shape[2]
    partner = routed_ref[:, k].reshape(size, RANK)
    return dot3((high_ref[k], low_ref[k]), split2(partner))


def side_kernel(facts_ref, high_ref, low_ref, routed_ref, side_ref):
    side_ref[...] = jnp.zeros_like(side_ref)
    for k in range(high_ref.shape[0]):

        @pl.when(facts_ref[LIVE + 2 * k + 1] != 0)
        def _():
            side_ref[...] = slot_product(high_ref, low_ref, routed_ref, k).reshape(side_ref.shape)


def couple_kernel(facts_ref, high_ref, low_ref, routed_ref, out_ref):
    for k in range(high_ref.shape[0]):
        live = facts_ref[LIVE + 2 * k].astype(F32)
        out_ref[k] = slot_product(high_ref, low_ref, routed_ref, k) * live


def merge_kernel(facts_ref, parts_ref, schur_ref, out_ref):
    first = facts_ref[FIRST] != 0
    side = parts_ref[0]
    for p in range(1, parts_ref.shape[0]):
        side = side + parts_ref[p]
    schur = schur_ref[...]
    out_ref[:, :RANK] = jnp.where(first, schur, side)
    out_ref[:, RANK:] = jnp.where(first, side, schur)


def shards(near_blocks, diag_block, bases, near_index, near_mask, parent_map):
    columns = lax.axis_size("col")
    clusters = lax.axis_size("clu")
    rows, size = bases.shape[1:]
    per_device = near_blocks.shape[1]
    shape = jax.ShapeDtypeStruct

    def shift(x, d):
        return lax.ppermute(x, "clu", [((i + d) % clusters, i) for i in range(clusters)])

    skeleton = pl.pallas_call(
        slice_kernel,
        out_shape=shape((rows, RANK), F32),
        in_specs=[HBM],
        out_specs=VMEM,
        scratch_shapes=[pltpu.SemaphoreType.DMA],
        compiler_params=params(4),
        name="skeleton",
    )(keep_out(bases[0]))
    far = shift(skeleton, clusters // 2)
    down8 = shift(skeleton, -8)
    down4 = shift(skeleton, -4)
    up4 = shift(skeleton, 4)
    chips = columns // 2
    spread = pl.pallas_call(
        spread_kernel,
        out_shape=pltpu.HBM((chips, 2 * rows, size), F32),
        in_specs=[HBM] * 2,
        out_specs=HBM,
        scratch_shapes=[pltpu.VMEM((2 * rows, size), F32), pltpu.SemaphoreType.DMA((chips,))],
        compiler_params=params(4),
        name="spread",
    )(keep_out(diag_block[0]), keep_out(bases[0]))
    same_core = [[2 * x + core for x in range(chips)] for core in range(2)]
    mine = lax.all_to_all(
        spread, "col", split_axis=0, concat_axis=0, axis_index_groups=same_core, tiled=False
    )
    theirs = lax.ppermute(mine, "col", [(c, c ^ 1) for c in range(columns)])
    near0 = jnp.stack([down8, down4, skeleton, up4])
    near2 = shift(near0, 2)
    near1 = shift(near0, 1)
    near3 = shift(near0, 3)
    facts = pl.pallas_call(
        facts_kernel,
        out_shape=shape((64,), jnp.int32),
        in_specs=[SMEM] * 3,
        out_specs=SMEM,
        name="facts",
    )(near_index.T, near_mask, parent_map)
    facts = keep_out(facts)
    ordered = pl.pallas_call(
        order_kernel,
        out_shape=pltpu.HBM((columns, per_device, rows, RANK), F32),
        in_specs=[SMEM] + [ANY] * 5,
        out_specs=HBM,
        compiler_params=params(2),
        scratch_shapes=[pltpu.SemaphoreType.DMA((near_index.shape[1],))],
        name="order",
    )(facts, near0, near1, near2, near3, far)
    routed = lax.all_to_all(ordered, "col", split_axis=0, concat_axis=0, tiled=False)
    count = RANK // columns
    high, low, schur, factor = pl.pallas_call(
        factor_kernel,
        out_shape=(
            shape((size, RANK), BF16),
            shape((size, RANK), BF16),
            shape((count, RANK), F32),
            shape(((size - RANK) // columns, size - RANK), F32),
        ),
        in_specs=[VMEM] * 2,
        out_specs=(VMEM,) * 4,
        scratch_shapes=[pltpu.VMEM((columns, 2 * rows, size), F32)]
        + [pltpu.VMEM((HALF, 2 * HALF), F32)] * 3
        + [pltpu.VMEM((RANK, RANK), F32)] * 2,
        cost_estimate=pl.CostEstimate(flops=6_000_000_000, bytes_accessed=4_000_000, transcendentals=0),
        compiler_params=params(24),
        name="factor",
    )(mine, theirs)
    projected = (per_device, RANK, size)
    rows_high, rows_low = pl.pallas_call(
        project_kernel,
        out_shape=(shape(projected, BF16),) * 2,
        in_specs=[HBM] + [VMEM] * 2,
        out_specs=(VMEM,) * 2,
        scratch_shapes=[
            pltpu.VMEM(near_blocks.shape[1:], F32),
            pltpu.SemaphoreType.DMA((per_device,)),
        ],
        cost_estimate=pl.CostEstimate(flops=1_000_000_000, bytes_accessed=4_000_000, transcendentals=0),
        compiler_params=params(16),
        name="project",
    )(keep_out(near_blocks[0]), high, low)
    side = pl.pallas_call(
        side_kernel,
        out_shape=shape((columns, count, RANK), F32),
        in_specs=[SMEM] + [VMEM] * 3,
        out_specs=VMEM,
        cost_estimate=pl.CostEstimate(flops=200_000_000, bytes_accessed=2_000_000, transcendentals=0),
        compiler_params=params(8),
        name="side",
    )(facts, rows_high, rows_low, routed)
    parts = lax.all_to_all(side, "col", split_axis=0, concat_axis=0, tiled=False)
    coupling = pl.pallas_call(
        couple_kernel,
        out_shape=shape((per_device, RANK, RANK), F32),
        in_specs=[SMEM] + [VMEM] * 3,
        out_specs=VMEM,
        cost_estimate=pl.CostEstimate(flops=400_000_000, bytes_accessed=4_000_000, transcendentals=0),
        compiler_params=params(8),
        name="couple",
    )(facts, rows_high, rows_low, routed)
    parent_rows = pl.pallas_call(
        merge_kernel,
        out_shape=shape((count, 2 * RANK), F32),
        in_specs=[SMEM] + [VMEM] * 2,
        out_specs=VMEM,
        compiler_params=params(4),
        name="merge",
    )(facts, parts, schur)
    return coupling[None], parent_rows[None], factor[None]


def solution(mesh):
    in_specs = (
        P("clu", "col", None, None),
        P("clu", "col", None),
        P("clu", "col", None),
        P(),
        P("clu", None),
        P(),
    )
    out_specs = (P("clu", "col", None, None), P("clu", "col", None), P("clu", "col", None))
    return jax.shard_map(shards, mesh=mesh, in_specs=in_specs, out_specs=out_specs, check_vma=False)
```

```python
import jax
import jax.numpy as jnp
from jax import lax
from jax.experimental import pallas as pl
from jax.experimental.pallas import tpu as pltpu
from jax.sharding import PartitionSpec as P


RANK = 256
HALF = 128
F32 = jnp.float32
BF16 = jnp.bfloat16
VMEM = pl.BlockSpec(memory_space=pltpu.VMEM)
SMEM = pl.BlockSpec(memory_space=pltpu.SMEM)
ANY = pl.BlockSpec(memory_space=pl.ANY)
HBM = pl.BlockSpec(memory_space=pltpu.HBM)


def dot_full(a, b, dims=((1,), (0,))):
    return lax.dot_general(
        a, b, (dims, ((), ())), precision=lax.Precision.HIGHEST, preferred_element_type=F32
    )


def split2(x):
    high = x.astype(BF16)
    return high, (x - high.astype(F32)).astype(BF16)


def dot3(a, b, dims=((1,), (0,))):
    def one(x, y):
        return lax.dot_general(x, y, (dims, ((), ())), preferred_element_type=F32)

    return one(a[0], b[0]) + (one(a[0], b[1]) + one(a[1], b[0]))


def split3(x):
    high = x.astype(BF16)
    rest = x - high.astype(F32)
    mid = rest.astype(BF16)
    return high, mid, (rest - mid.astype(F32)).astype(BF16)


def factor_half(work, upper):
    sub = lax.broadcasted_iota(jnp.int32, (8, HALF), 0)

    def spread_lane(x, j):
        return jnp.broadcast_to(x[:, j : j + 1], (8, HALF))

    def spread_row(x, m):
        return jnp.broadcast_to(x[m : m + 1, :], (8, HALF))

    rows_a, rows_w = work[0:8, :HALF], work[0:8, HALF:]
    for group in range(HALF // 8):
        base = 8 * group
        columns = [spread_lane(rows_a, base + j) for j in range(8)]
        cell = {(m, j): spread_row(columns[j], m) for j in range(8) for m in range(j, 8)}
        inv = [None] * 8
        ratio = {}
        for k in range(8):
            inv[k] = 1.0 / cell[k, k]
            for m in range(k + 1, 8):
                ratio[m, k] = cell[m, k] * inv[k]
            for j in range(k + 1, 8):
                for m in range(j, 8):
                    cell[m, j] = cell[m, j] - ratio[m, k] * cell[j, k]
        ra = [spread_row(rows_a, m) for m in range(8)]
        rw = [spread_row(rows_w, m) for m in range(8)]
        for m in range(8):
            for k in range(m):
                ra[m] = ra[m] - ratio[m, k] * ra[k]
                rw[m] = rw[m] - ratio[m, k] * rw[k]
        ua = uw = None
        for m in range(8):
            scale = lax.rsqrt(cell[m, m])
            a, w = ra[m] * scale, rw[m] * scale
            ua = a if ua is None else jnp.where(sub == m, a, ua)
            uw = w if uw is None else jnp.where(sub == m, w, uw)
        upper[base : base + 8, :HALF] = ua
        upper[base : base + 8, HALF:] = uw
        after = base + 8
        if after == HALF:
            break
        next_a, next_w = work[after : after + 8, :HALF], work[after : after + 8, HALF:]
        lead = [spread_lane(next_a, base + k) for k in range(8)]
        for k in range(8):
            for j in range(k):
                lead[k] = lead[k] - lead[j] * ratio[k, j]
        for k in range(8):
            factor = lead[k] * inv[k]
            next_a = next_a - factor * ra[k]
            next_w = next_w - factor * rw[k]
        rows_a, rows_w = next_a, next_w
        low = after + 8
        if low < HALF:
            h, m, l = (x.astype(F32) for x in split3(jnp.concatenate([ua, uw], axis=1)))
            ha, ma, la = h[:, :HALF], m[:, :HALF], l[:, :HALF]
            left = jnp.concatenate([ha, ha, ma, ha, la, ma], axis=0).astype(BF16)
            right = jnp.concatenate([h, m, h, l, h, m], axis=0).astype(BF16)
            step = lax.dot_general(left, right, (((0,), (0,)), ((), ())), preferred_element_type=F32)
            work[low:, :] = work[low:, :] - step[low:, :]


def params(mib):
    return pltpu.CompilerParams(vmem_limit_bytes=mib * 2**20)


def keep_out(x):
    return pltpu.with_memory_space_constraint(x, pltpu.HBM)


def slice_kernel(bases_ref, skeleton_ref, sem):
    source = bases_ref.at[:, pl.ds(bases_ref.shape[1] - RANK, RANK)]
    run_copies([pltpu.make_async_copy(source, skeleton_ref, sem)])


def run_copies(copies):
    for copy in copies:
        copy.start()
    for copy in copies:
        copy.wait()


def find_sibling(own, parent_ref):
    parent = parent_ref[own]

    def step(i, found):
        return jnp.where((parent_ref[i] == parent) & (i != own), i, found)

    return lax.fori_loop(0, parent_ref.shape[0], step, jnp.int32(0), unroll=True)


FIRST, LIVE = 32, 33


def spread_kernel(diag_ref, bases_ref, out_ref, both, sem):
    rows = diag_ref.shape[0]
    pair = (diag_ref, bases_ref)
    run_copies(
        [pltpu.make_async_copy(ref, both.at[pl.ds(q * rows, rows)], sem.at[q]) for q, ref in enumerate(pair)]
    )
    run_copies([pltpu.make_async_copy(both, out_ref.at[p], sem.at[p]) for p in range(out_ref.shape[0])])


def facts_kernel(index_ref, mask_ref, parent_ref, facts_ref):
    own, column = lax.axis_index("clu"), lax.axis_index("col")
    slots, clusters = index_ref.shape
    half = slots // 2
    for k in range(slots):
        offset = (index_ref[k, own] - own + clusters + half) % clusters
        facts_ref[jnp.where(offset < slots, offset, half)] = k
    sibling = find_sibling(own, parent_ref)
    facts_ref[FIRST] = (own < sibling).astype(jnp.int32)
    count = slots // lax.axis_size("col")
    for k in range(count):
        slot = column * count + k
        live = mask_ref[0, slot]
        facts_ref[LIVE + 2 * k] = live
        facts_ref[LIVE + 2 * k + 1] = jnp.where(index_ref[slot, own] == sibling, live, 0)


def order_kernel(facts_ref, near0, near1, near2, near3, far, out_ref, sem):
    stacks = (near0, near1, near2, near3)
    copies = []
    for d in range(16):
        slot = facts_ref[d]
        source = far if d == 8 else stacks[d % 4].at[d // 4]
        copies.append(pltpu.make_async_copy(source, out_ref.at[slot // 2, slot % 2], sem.at[d]))
    run_copies(copies)


def factor_kernel(
    mine_ref, theirs_ref, high_ref, low_ref, schur_ref, factor_ref, db_ref, work, upper1, upper2, full, solve_ref
):
    core = lax.axis_index("col") % 2
    for x in range(mine_ref.shape[0]):
        db_ref[2 * x + core] = mine_ref[x]
        db_ref[2 * x + 1 - core] = theirs_ref[x]
    rows = db_ref.shape[1] // 2
    size = db_ref.shape[0] * rows
    diag = db_ref[:, :rows, :].reshape(size, size)
    basis = db_ref[:, rows:, :].reshape(size, size)
    first = ((0,), (0,))
    red = size - RANK
    reduced = dot_full(dot_full(diag, basis[:, :red]), basis, first)
    skeleton = split2(basis[:, red:])
    corner = dot3(skeleton, split2(dot3(split2(diag), skeleton)), first)
    ri = lax.broadcasted_iota(jnp.int32, (HALF, HALF), 0)
    ci = lax.broadcasted_iota(jnp.int32, (HALF, HALF), 1)
    eye = (ri == ci).astype(F32)
    work[:, :HALF] = reduced[:HALF, :HALF]
    work[:, HALF:] = eye
    factor_half(work, upper1)
    inv1 = upper1[:, HALF:]
    top = dot_full(inv1, reduced[:HALF, HALF:])
    low_t = top[:, :HALF]
    rest = reduced[HALF:red, HALF:] - dot_full(low_t, top, first)
    work[:, :HALF] = rest[:, :HALF]
    work[:, HALF:] = eye
    factor_half(work, upper2)
    inv2 = upper2[:, HALF:]
    couple1 = top[:, HALF:]
    joint = dot_full(inv2, jnp.concatenate([rest[:, HALF:], dot_full(low_t, inv1, first)], axis=1))
    couple2, cross = joint[:, :RANK], joint[:, RANK:]
    solve_ref[:HALF, :] = dot_full(inv1, couple1, first) - dot_full(cross, couple2, first)
    solve_ref[HALF:, :] = dot_full(inv2, couple2, first)
    lift = basis[:, red:] - dot3(split2(basis[:, :red]), split2(solve_ref[...]))
    high_ref[...], low_ref[...] = split2(lift)
    column = lax.axis_index("col")
    count = schur_ref.shape[0]
    start = pl.multiple_of(column * count, count)
    full[...] = corner - (
        dot_full(couple1, couple1, first) + dot_full(couple2, couple2, first)
    )
    schur_ref[...] = full[pl.ds(start, count), :]
    full[:HALF, :HALF] = jnp.where(ri >= ci, upper1[:, :HALF].T, 0.0)
    full[HALF:, :HALF] = low_t.T
    full[:HALF, HALF:] = jnp.zeros((HALF, HALF), F32)
    full[HALF:, HALF:] = jnp.where(ri >= ci, upper2[:, :HALF].T, 0.0)
    factor_ref[...] = full[pl.ds(start, count), :]


def project_kernel(near_ref, high_ref, low_ref, out_high, out_low, block, sem):
    count = near_ref.shape[0]
    loads = [pltpu.make_async_copy(near_ref.at[k], block.at[k], sem.at[k]) for k in range(count)]
    for load in loads:
        load.start()
    lift = high_ref[...], low_ref[...]
    for k in range(count):
        loads[k].wait()
        out_high[k], out_low[k] = split2(dot3(lift, split2(block[k]), ((0,), (0,))))


def slot_product(high_ref, low_ref, routed_ref, k):
    size = high_ref.shape[2]
    partner = routed_ref[:, k].reshape(size, RANK)
    return dot3((high_ref[k], low_ref[k]), split2(partner))


def side_kernel(facts_ref, high_ref, low_ref, routed_ref, side_ref):
    side_ref[...] = jnp.zeros_like(side_ref)
    for k in range(high_ref.shape[0]):

        @pl.when(facts_ref[LIVE + 2 * k + 1] != 0)
        def _():
            side_ref[...] = slot_product(high_ref, low_ref, routed_ref, k).reshape(side_ref.shape)


def couple_kernel(facts_ref, high_ref, low_ref, routed_ref, out_ref):
    for k in range(high_ref.shape[0]):
        live = facts_ref[LIVE + 2 * k].astype(F32)
        out_ref[k] = slot_product(high_ref, low_ref, routed_ref, k) * live


def merge_kernel(facts_ref, parts_ref, schur_ref, out_ref):
    first = facts_ref[FIRST] != 0
    side = parts_ref[0]
    for p in range(1, parts_ref.shape[0]):
        side = side + parts_ref[p]
    schur = schur_ref[...]
    out_ref[:, :RANK] = jnp.where(first, schur, side)
    out_ref[:, RANK:] = jnp.where(first, side, schur)


def shards(near_blocks, diag_block, bases, near_index, near_mask, parent_map):
    columns = lax.axis_size("col")
    clusters = lax.axis_size("clu")
    rows, size = bases.shape[1:]
    per_device = near_blocks.shape[1]
    shape = jax.ShapeDtypeStruct

    def shift(x, d):
        return lax.ppermute(x, "clu", [((i + d) % clusters, i) for i in range(clusters)])

    def quarter_turn(x):
        step = clusters // 4
        pairs = [
            ((i + (step if c % 2 == 0 else -step)) % clusters * columns + c, i * columns + c)
            for i in range(clusters)
            for c in range(columns)
        ]
        return lax.ppermute(x, ("clu", "col"), pairs)

    skeleton = pl.pallas_call(
        slice_kernel,
        out_shape=shape((rows, RANK), F32),
        in_specs=[HBM],
        out_specs=VMEM,
        scratch_shapes=[pltpu.SemaphoreType.DMA],
        compiler_params=params(4),
        name="skeleton",
    )(keep_out(bases[0]))
    halfway = quarter_turn(skeleton)
    far = quarter_turn(halfway)
    down8 = shift(skeleton, -8)
    down4 = shift(skeleton, -4)
    up4 = shift(skeleton, 4)
    chips = columns // 2
    spread = pl.pallas_call(
        spread_kernel,
        out_shape=pltpu.HBM((chips, 2 * rows, size), F32),
        in_specs=[HBM] * 2,
        out_specs=HBM,
        scratch_shapes=[pltpu.VMEM((2 * rows, size), F32), pltpu.SemaphoreType.DMA((chips,))],
        compiler_params=params(4),
        name="spread",
    )(keep_out(diag_block[0]), keep_out(bases[0]))
    same_core = [[2 * x + core for x in range(chips)] for core in range(2)]
    mine = lax.all_to_all(
        spread, "col", split_axis=0, concat_axis=0, axis_index_groups=same_core, tiled=False
    )
    theirs = lax.ppermute(mine, "col", [(c, c ^ 1) for c in range(columns)])
    near0 = jnp.stack([down8, down4, skeleton, up4])
    near2 = shift(near0, 2)
    near1 = shift(near0, 1)
    near3 = shift(near0, 3)
    facts = pl.pallas_call(
        facts_kernel,
        out_shape=shape((64,), jnp.int32),
        in_specs=[SMEM] * 3,
        out_specs=SMEM,
        name="facts",
    )(near_index.T, near_mask, parent_map)
    facts = keep_out(facts)
    ordered = pl.pallas_call(
        order_kernel,
        out_shape=pltpu.HBM((columns, per_device, rows, RANK), F32),
        in_specs=[SMEM] + [ANY] * 5,
        out_specs=HBM,
        compiler_params=params(2),
        scratch_shapes=[pltpu.SemaphoreType.DMA((near_index.shape[1],))],
        name="order",
    )(facts, near0, near1, near2, near3, far)
    routed = lax.all_to_all(ordered, "col", split_axis=0, concat_axis=0, tiled=False)
    count = RANK // columns
    high, low, schur, factor = pl.pallas_call(
        factor_kernel,
        out_shape=(
            shape((size, RANK), BF16),
            shape((size, RANK), BF16),
            shape((count, RANK), F32),
            shape(((size - RANK) // columns, size - RANK), F32),
        ),
        in_specs=[VMEM] * 2,
        out_specs=(VMEM,) * 4,
        scratch_shapes=[pltpu.VMEM((columns, 2 * rows, size), F32)]
        + [pltpu.VMEM((HALF, 2 * HALF), F32)] * 3
        + [pltpu.VMEM((RANK, RANK), F32)] * 2,
        cost_estimate=pl.CostEstimate(flops=6_000_000_000, bytes_accessed=4_000_000, transcendentals=0),
        compiler_params=params(24),
        name="factor",
    )(mine, theirs)
    projected = (per_device, RANK, size)
    rows_high, rows_low = pl.pallas_call(
        project_kernel,
        out_shape=(shape(projected, BF16),) * 2,
        in_specs=[HBM] + [VMEM] * 2,
        out_specs=(VMEM,) * 2,
        scratch_shapes=[
            pltpu.VMEM(near_blocks.shape[1:], F32),
            pltpu.SemaphoreType.DMA((per_device,)),
        ],
        cost_estimate=pl.CostEstimate(flops=1_000_000_000, bytes_accessed=4_000_000, transcendentals=0),
        compiler_params=params(16),
        name="project",
    )(keep_out(near_blocks[0]), high, low)
    side = pl.pallas_call(
        side_kernel,
        out_shape=shape((columns, count, RANK), F32),
        in_specs=[SMEM] + [VMEM] * 3,
        out_specs=VMEM,
        cost_estimate=pl.CostEstimate(flops=200_000_000, bytes_accessed=2_000_000, transcendentals=0),
        compiler_params=params(8),
        name="side",
    )(facts, rows_high, rows_low, routed)
    parts = lax.all_to_all(side, "col", split_axis=0, concat_axis=0, tiled=False)
    coupling = pl.pallas_call(
        couple_kernel,
        out_shape=shape((per_device, RANK, RANK), F32),
        in_specs=[SMEM] + [VMEM] * 3,
        out_specs=VMEM,
        cost_estimate=pl.CostEstimate(flops=400_000_000, bytes_accessed=4_000_000, transcendentals=0),
        compiler_params=params(8),
        name="couple",
    )(facts, rows_high, rows_low, routed)
    parent_rows = pl.pallas_call(
        merge_kernel,
        out_shape=shape((count, 2 * RANK), F32),
        in_specs=[SMEM] + [VMEM] * 2,
        out_specs=VMEM,
        compiler_params=params(4),
        name="merge",
    )(facts, parts, schur)
    return coupling[None], parent_rows[None], factor[None]


def solution(mesh):
    in_specs = (
        P("clu", "col", None, None),
        P("clu", "col", None),
        P("clu", "col", None),
        P(),
        P("clu", None),
        P(),
    )
    out_specs = (P("clu", "col", None, None), P("clu", "col", None), P("clu", "col", None))
    return jax.shard_map(shards, mesh=mesh, in_specs=in_specs, out_specs=out_specs, check_vma=False)
```
